32 devices in a mesh: grp: 1, ep: 32 (over z, y, x, core).
Axes of the slice: x: 2, y: 2, z: 4, core: 2. Of those that a mesh axis runs over, the one named last changes fastest.
Arguments:
- hidden_states: bfloat16 [192, 3584], P(('grp', 'ep')), may hold values from -6 to 6
- norm_gain: float32 [3584], replicated, may hold values from 0.1 to 1.9
- gate_scores: float32 [192, 8], P(('grp', 'ep')), may hold values from 0.05 to 1
- routes: int32 [192, 8], P(('grp', 'ep')), may hold values from 0 to 15, all different within a row; in each aligned block of 6 rows (0 to 5, 6 to 11, ...) at most 6 rows name the same one
- draft_counts: int32 [64], P(('grp', 'ep')), may hold values from 1 to 2
- w_gate: bfloat16 [32, 3584, 512], P('ep'), may hold values from -0.09375 to 0.09375
- w_up: bfloat16 [32, 3584, 512], P('ep'), may hold values from -0.09375 to 0.09375
- w_down: bfloat16 [32, 512, 3584], P('ep'), may hold values from -0.1875 to 0.1875
Outputs:
- moe_out: bfloat16 [192, 3584], P(('grp', 'ep'))
The draws below stay inside these ranges and needn't reach their ends.
Inputs may be any that keep to these rules, and one draw needn't show every extreme that they name: `routes`: each token slot names 8 different experts; among the 6 token slots of one device no expert is named more than 6 times.
All inputs are finite; a program needn't handle non-finite values.
Results may differ from the reference program's by a relative error of at most 0.0077.
Values may be sent and summed in bfloat16 or wider, within the bound.
No kernel may reach another device: no remote copies, remote signals or barrier semaphores. Data moves between devices by JAX's collectives and lax.ppermute only.
A program may use at most 64 MiB of HBM per device.

```python
import math
import jax
import jax.numpy as jnp
import numpy as np
from jax import lax

D = 3584
FF = 1024
FF_DEV = 512
TOPK = 8
SLOTS = 3
ROWS = 64
TOK_DEV = 6
TOKENS = 192
EXPERTS = 16
CAP = 6
N_EP = 32


def plant(entries, stream_key, low, high):
    longest = entries.shape.index(max(entries.shape))
    spots = []
    for shift in (0, 1):
        where = [jax.random.randint(jax.random.fold_in(stream_key, axis), (), 0, length) for axis, length in enumerate(entries.shape)]
        where[longest] = (where[longest] + shift) % entries.shape[longest]
        spots.append(tuple(where))
    return entries.at[spots[0]].set(low).at[spots[1]].set(high)


def shard_levels(key, extent, cuts, smallest, high):
    def one(dim, parts):
        draws = jax.random.uniform(jax.random.fold_in(jax.random.fold_in(key, 6), dim), (parts,), jnp.float32, smallest / len(cuts), high / len(cuts))
        return jnp.repeat(jnp.exp(draws), extent[dim] // parts).reshape((-1,) + (1,) * (len(extent) - dim - 1))

    factor_of = one(*cuts[0])
    for cut in cuts[1:]:
        factor_of = factor_of * one(*cut)
    return factor_of


def deal_out(key, own, number, rows, amount, top, bound, slope):
    ranking = jax.random.permutation(key, amount)
    crowded, common = load_shares(amount, rows * top, bound, slope, True), load_shares(amount, rows * top, bound, slope, False)
    places = jnp.arange(amount)

    def named(sizes, rotation):
        used = int((sizes > 0).sum())
        fixed = max(1, used // 4)
        passed = fixed + (places - fixed + rotation * (used - fixed)) % max(1, amount - fixed)
        return jnp.zeros((amount,), jnp.int32).at[ranking[jnp.where(places < fixed, places, passed)]].set(jnp.asarray(sizes, jnp.int32))

    sizes = jnp.where(number % 4 == 0, named(crowded, number // 4), named(common, number - number // 4 - 1))
    mixed = jax.random.permutation(jax.random.fold_in(own, 3), amount)
    donor, receiver = mixed[0:amount // 2 * 2:2], mixed[1:amount // 2 * 2:2]
    margin = jnp.minimum(sizes[donor] - 1, bound - sizes[receiver]) // 2
    margin = jnp.where((donor == ranking[0]) | (receiver == ranking[0]) | (sizes[receiver] == 0), 0, jnp.maximum(margin, 0))
    passed = jax.random.randint(jax.random.fold_in(own, 4), (amount // 2,), 0, 1 << 20) % (margin + 1)
    sizes = sizes.at[donor].add(-passed).at[receiver].add(passed)
    labels = jnp.searchsorted(jnp.cumsum(sizes), jnp.arange(rows * top), side="right").astype(jnp.int32)
    table = labels.reshape(top, rows).T
    table = table[jax.random.permutation(jax.random.fold_in(own, 1), rows)]
    rotation = jax.random.randint(jax.random.fold_in(own, 2), (rows, 1), 0, top)
    return jnp.take_along_axis(table, (jnp.arange(top)[None, :] + rotation) % top, axis=1)


def load_shares(number_of, total, reach, slope, full):
    loads = [(1 << 20) // math.isqrt(grade ** slope) + 1 for grade in range(1, number_of + 1)]
    largest = reach if full else min(reach, max(-(-total // number_of), total * loads[0] // sum(loads)))
    least = 1 if total - largest >= number_of - 1 else 0
    given, surplus = [largest] + [least] * (number_of - 1), total - largest - least * (number_of - 1)
    while surplus > 0:
        free = [i for i in range(1, number_of) if given[i] < largest] or [i for i in range(1, number_of) if given[i] < reach]
        whole, remaining = sum([loads[i] for i in free]), surplus
        for i in free:
            extra = min(reach - given[i], max(1, remaining * loads[i] // whole), surplus)
            given[i] = given[i] + extra
            surplus = surplus - extra
    return np.array(given)


def bell_draw(key, shape, spread, limit, pieces=(), held_as=jnp.bfloat16):
    result = jax.random.normal(key, shape, jnp.float32) * spread
    if len(pieces) > 0:
        result = shard_levels(key, shape, pieces, -0.22, 0.18) * result
    return jnp.clip(result, min=-limit, max=limit).astype(held_as)


def setup_inputs(seed: int = 0, part: int = 0) -> dict:
    key_list = jax.random.split(jax.random.key(seed), 9)
    part_keys = jax.random.split(jax.random.fold_in(key_list[8], part), 9)
    hidden_states = bell_draw(part_keys[0], (TOKENS, D), 1.0, 6.0, ((0, 32),))
    norm_gain = jnp.clip(1.0 + 0.18 * jax.random.normal(key_list[1], (D,), jnp.float32), 0.1, 1.9)
    gate_scores = jnp.clip(jnp.exp(math.log(1.0) - 2.9957323 * jax.random.uniform(part_keys[2], (TOKENS, TOPK), jnp.float32) ** shard_levels(part_keys[2], (TOKENS, TOPK), ((0, 32),), -0.2, 0.2)), 0.05, 1.0)
    routes_keys = jax.random.split(jax.random.fold_in(part_keys[3], 1), TOKENS // TOK_DEV)
    routes_turns = jax.random.permutation(jax.random.fold_in(part_keys[3], 3), TOKENS // TOK_DEV)
    routes = jax.vmap(lambda own, number: deal_out(jax.random.fold_in(part_keys[3], 2), own, number, TOK_DEV, EXPERTS, TOPK, CAP, 2))(routes_keys, routes_turns).reshape((TOKENS, TOPK))
    draft_counts = plant(jax.random.randint(part_keys[4], (ROWS,), 1, 3), jax.random.fold_in(part_keys[4], 1), 1, 2).astype(jnp.int32)
    w_gate = bell_draw(key_list[5], (N_EP, D, FF_DEV), D ** -0.5, 0.09375, ((0, 32),))
    w_up = bell_draw(key_list[6], (N_EP, D, FF_DEV), D ** -0.5, 0.09375, ((0, 32),))
    w_down = bell_draw(key_list[7], (N_EP, FF_DEV, D), FF ** -0.5, 0.1875, ((0, 32),))
    return dict(hidden_states=hidden_states, norm_gain=norm_gain, gate_scores=gate_scores, routes=routes, draft_counts=draft_counts, w_gate=w_gate, w_up=w_up, w_down=w_down)


def expert_half(chosen, gate_half, up_half, down_half):
    gate_proj = jnp.dot(chosen, gate_half, preferred_element_type=jnp.float32)
    up_proj = jnp.dot(chosen, up_half, preferred_element_type=jnp.float32)
    hidden = (jax.nn.silu(gate_proj) * up_proj).astype(jnp.bfloat16)
    return jnp.dot(hidden, down_half, preferred_element_type=jnp.float32).astype(jnp.bfloat16)

def reference(hidden_states, norm_gain, gate_scores, routes, draft_counts, w_gate, w_up, w_down):
    position = jnp.arange(TOKENS) % SLOTS
    live_mask = (position <= jnp.repeat(draft_counts, SLOTS)).astype(jnp.float32)
    wide_states = hidden_states.astype(jnp.float32)
    mean_square = lax.optimization_barrier(jnp.mean(wide_states * wide_states, axis=-1, keepdims=True))
    normed = (wide_states * lax.rsqrt(mean_square + 1e-06) * norm_gain).astype(jnp.bfloat16)
    gate_weights = 2.5 * gate_scores / lax.optimization_barrier(jnp.sum(gate_scores, axis=-1, keepdims=True))
    expert_ids = jnp.arange(EXPERTS)
    coefficient = lax.optimization_barrier(jnp.sum((routes[:, :, None] == expert_ids[None, None, :]).astype(jnp.float32) * gate_weights[:, :, None], axis=1)) * live_mask[:, None]
    slot_limit = N_EP * CAP

    def one_expert(running, expert):
        column = lax.dynamic_index_in_dim(coefficient, expert, axis=1, keepdims=False)
        picked = jnp.nonzero(column > 0, size=slot_limit, fill_value=0)[0].astype(jnp.int32)
        filled = jnp.sum((column > 0).astype(jnp.int32))
        chosen = normed[picked]
        first_part = expert_half(chosen, w_gate[2 * expert], w_up[2 * expert], w_down[2 * expert])
        second_part = expert_half(chosen, w_gate[2 * expert + 1], w_up[2 * expert + 1], w_down[2 * expert + 1])
        expert_out = (first_part.astype(jnp.float32) + second_part.astype(jnp.float32)).astype(jnp.bfloat16)
        weight = jnp.where(jnp.arange(slot_limit) < filled, column[picked], jnp.zeros((slot_limit,), jnp.float32))
        running = running.at[picked].add(weight[:, None] * expert_out.astype(jnp.float32))
        return (running, None)
    running, unused = lax.scan(one_expert, jnp.zeros((TOKENS, D), jnp.float32), jnp.arange(EXPERTS))
    return running.astype(jnp.bfloat16)
```

```python
import jax
import jax.numpy as jnp
from jax import lax
from jax.experimental import pallas as pl
from jax.experimental.pallas import tpu as pltpu
from jax.sharding import PartitionSpec as P

VMEM = pl.BlockSpec(memory_space=pltpu.VMEM)
SMEM = pl.BlockSpec(memory_space=pltpu.SMEM)
MIB = 1024 * 1024


def swapped(array, distance):
    size = lax.axis_size("ep")
    return lax.ppermute(array, "ep", [(i, i ^ distance) for i in range(size)])


def lane_round(count):
    return -(-count // 128) * 128


def call(kernel, outs, limit, *args, specs=None, flops=0):
    moved = sum(a.size * a.dtype.itemsize for a in (*args, *outs))
    single = len(outs) == 1
    return pl.pallas_call(
        kernel,
        out_shape=outs[0] if single else tuple(outs),
        in_specs=specs or [VMEM] * len(args),
        out_specs=VMEM if single else tuple([VMEM] * len(outs)),
        compiler_params=pltpu.CompilerParams(vmem_limit_bytes=limit),
        cost_estimate=pl.CostEstimate(flops=flops, bytes_accessed=moved, transcendentals=0),
    )(*args)


def pack_kernel(draft_ref, states_ref, gain_ref, scores_ref, routes_ref, out_ref):
    tokens, width = states_ref.shape
    half = width // 2
    extra = out_ref.shape[2] - half
    requests = draft_ref.shape[0]
    slots = tokens // requests
    wide = states_ref[...].astype(jnp.float32)
    mean_square = jnp.mean(wide * wide, axis=-1, keepdims=True)
    normed = (wide * lax.rsqrt(mean_square + 1e-06) * gain_ref[...]).astype(jnp.bfloat16)
    scores = scores_ref[...]
    weights = 2.5 * scores / jnp.sum(scores, axis=-1, keepdims=True)
    row = lax.broadcasted_iota(jnp.int32, (tokens, 1), 0)
    live = jnp.zeros((tokens, 1), jnp.bool_)
    for request in range(requests):
        inside = (row >= request * slots) & (row <= request * slots + draft_ref[request])
        live = live | (inside & (row < (request + 1) * slots))
    weights = jnp.where(live, weights, 0.0)
    lane = lax.broadcasted_iota(jnp.int32, (tokens, extra), 1)
    coefficient = jnp.zeros((tokens, extra), jnp.float32)
    for k in range(routes_ref.shape[1]):
        coefficient += jnp.where(routes_ref[:, k : k + 1] == lane, weights[:, k : k + 1], 0.0)
    coarse = coefficient.astype(jnp.bfloat16)
    fine = (coefficient - coarse.astype(jnp.float32)).astype(jnp.bfloat16)
    out_ref[0, :, :half] = normed[:, :half]
    out_ref[1, :, :half] = normed[:, half:]
    out_ref[0, :, half:] = coarse
    out_ref[1, :, half:] = fine


def spread_kernel(own_ref, other_ref, out_ref):
    pieces = [own_ref[0], other_ref[0], own_ref[1], other_ref[1]]
    rows = jnp.concatenate([p.astype(jnp.float32) for p in pieces], axis=0).astype(jnp.bfloat16)
    for j in range(out_ref.shape[0]):
        out_ref[j] = rows


def expert_kernel(
    expert_ref, own_ref, other_ref, gate_ref, up_ref, down_ref, keep_ref, give_ref
):
    half = gate_ref.shape[1] // 2
    count = own_ref.shape[1] // 2
    rows = own_ref.shape[0] * count

    def gathered(part):
        pieces = []
        for ref in (own_ref, other_ref):
            for j in range(ref.shape[0]):
                pieces.append(ref[j, part * count : (part + 1) * count, :].astype(jnp.float32))
        return jnp.concatenate(pieces, axis=0)

    low, high = gathered(0), gathered(1)
    mixed = low[:, half:] + high[:, half:]
    lane = lax.broadcasted_iota(jnp.int32, mixed.shape, 1)
    coefficient = jnp.sum(jnp.where(lane == expert_ref[0], mixed, 0.0), axis=1, keepdims=True)
    low = low[:, :half].astype(jnp.bfloat16)
    high = high[:, :half].astype(jnp.bfloat16)

    def projected(ref):
        first = jnp.dot(low, ref[0, :half], preferred_element_type=jnp.float32)
        return first + jnp.dot(high, ref[0, half:], preferred_element_type=jnp.float32)

    gate = projected(gate_ref)
    up = projected(up_ref)
    hidden = (gate / (1.0 + jnp.exp(-gate)) * up).astype(jnp.bfloat16)
    step = down_ref.shape[2] // 7
    for start in range(0, down_ref.shape[2], step):
        columns = slice(start, start + step)
        partial = jnp.dot(hidden, down_ref[0, :, columns], preferred_element_type=jnp.float32)
        partial = partial * coefficient
        keep_ref[:, columns] = partial[:rows]
        give_ref[:, columns] = partial[rows:].astype(jnp.bfloat16)


def fold_kernel(keep_ref, other_ref, out_ref):
    half = keep_ref.shape[1] // 2
    count = out_ref.shape[1] // 2
    for j in range(out_ref.shape[0]):
        rows = slice(j * count, (j + 1) * count)
        total = keep_ref[rows, :] + other_ref[rows, :].astype(jnp.float32)
        both = jnp.concatenate([total[:, :half], total[:, half:]], axis=0)
        out_ref[j] = both.astype(jnp.bfloat16)


def sum_kernel(parts_ref, keep_ref, give_ref):
    half = keep_ref.shape[1] // 2
    tokens = keep_ref.shape[0]
    total = parts_ref[0].astype(jnp.float32)
    for j in range(1, parts_ref.shape[0]):
        total += parts_ref[j].astype(jnp.float32)
    keep_ref[:, :half] = total[:tokens]
    keep_ref[:, half:] = total[2 * tokens : 3 * tokens]
    give_ref[:, :half] = total[tokens : 2 * tokens].astype(jnp.bfloat16)
    give_ref[:, half:] = total[3 * tokens :].astype(jnp.bfloat16)


def finish_kernel(keep_ref, other_ref, out_ref):
    out_ref[...] = (keep_ref[...] + other_ref[...].astype(jnp.float32)).astype(jnp.bfloat16)


def body(hidden_states, norm_gain, gate_scores, routes, draft_counts, w_gate, w_up, w_down):
    tokens, width = hidden_states.shape
    devices = lax.axis_size("ep")
    members = devices // 4
    far = devices // 2
    groups = [
        [2 * m + core + side * far for m in range(members)] for side in range(2) for core in range(2)
    ]
    half = width // 2
    carried = half + lane_round(devices // 2)
    shape = jax.ShapeDtypeStruct
    bf16, f32 = jnp.bfloat16, jnp.float32
    packed = call(
        pack_kernel,
        [shape((2, tokens, carried), bf16)],
        2 * MIB,
        draft_counts,
        hidden_states,
        norm_gain.reshape(1, width),
        gate_scores,
        routes,
        specs=[SMEM] + [VMEM] * 4,
    )
    spread = call(
        spread_kernel,
        [shape((members, 4 * tokens, carried), bf16)],
        8 * MIB,
        packed,
        swapped(packed, far),
    )

    def exchanged(array):
        return lax.all_to_all(
            array, "ep", split_axis=0, concat_axis=0, axis_index_groups=groups, tiled=True
        )

    own = exchanged(spread)
    other = swapped(own, 1)
    rows = members * 2 * tokens
    expert = (lax.axis_index("ep") // 2).astype(jnp.int32).reshape(1)
    keep, give = call(
        expert_kernel,
        [shape((rows, width), f32), shape((rows, width), bf16)],
        48 * MIB,
        expert,
        own,
        other,
        w_gate,
        w_up,
        w_down,
        specs=[SMEM] + [VMEM] * 5,
        flops=12 * rows * width * w_gate.shape[2],
    )
    folded = call(
        fold_kernel,
        [shape((members, 4 * tokens, half), bf16)],
        20 * MIB,
        keep,
        swapped(give, 1),
    )
    keep, give = call(
        sum_kernel,
        [shape((tokens, width), f32), shape((tokens, width), bf16)],
        8 * MIB,
        exchanged(folded),
    )
    return call(
        finish_kernel, [shape((tokens, width), bf16)], 2 * MIB, keep, swapped(give, far)
    )


def solution(mesh):
    return jax.shard_map(
        body,
        mesh=mesh,
        in_specs=(
            P(("grp", "ep"), None),
            P(),
            P(("grp", "ep"), None),
            P(("grp", "ep"), None),
            P(("grp", "ep")),
            P("ep", None, None),
            P("ep", None, None),
            P("ep", None, None),
        ),
        out_specs=P(("grp", "ep"), None),
        check_vma=False,
    )
```

```python
import math

import jax
import jax.numpy as jnp
from jax import lax
from jax.experimental import pallas as pl
from jax.experimental.pallas import tpu as pltpu
from jax.sharding import PartitionSpec as P

VMEM = pl.BlockSpec(memory_space=pltpu.VMEM)
ANY = pl.BlockSpec(memory_space=pl.ANY)
HBM = pl.BlockSpec(memory_space=pltpu.HBM)
MIB = 1024 * 1024


def swapped(array, distance):
    size = lax.axis_size("ep")
    return lax.ppermute(array, "ep", [(i, i ^ distance) for i in range(size)])


def lane_round(count):
    return -(-count // 128) * 128


def call(kernel, outs, limit, *args, specs=None, flops=0, scratch=()):
    moved = sum(math.prod(a.shape) * a.dtype.itemsize for a in (*args, *outs))
    single = len(outs) == 1
    return pl.pallas_call(
        kernel,
        out_shape=outs[0] if single else tuple(outs),
        in_specs=specs or [VMEM] * len(args),
        out_specs=VMEM if single else tuple([VMEM] * len(outs)),
        scratch_shapes=list(scratch),
        compiler_params=pltpu.CompilerParams(vmem_limit_bytes=limit),
        cost_estimate=pl.CostEstimate(flops=flops, bytes_accessed=moved, transcendentals=0),
    )(*args)


def pack_kernel(
    draft_hbm, states_hbm, gain_hbm, scores_hbm, routes_hbm, out_ref,
    draft_ref, states_ref, gain_ref, scores_ref, routes_ref, sems,
):
    sources = (draft_hbm, states_hbm, gain_hbm, scores_hbm, routes_hbm)
    targets = (draft_ref, states_ref, gain_ref, scores_ref, routes_ref)
    copies = [
        pltpu.make_async_copy(source, target, sems.at[i])
        for i, (source, target) in enumerate(zip(sources, targets))
    ]
    for copy in copies:
        copy.start()
    for copy in copies:
        copy.wait()
    tokens, width = states_ref.shape
    half = width // 2
    extra = out_ref.shape[2] - half
    requests = draft_ref.shape[0]
    slots = tokens // requests
    wide = states_ref[...].astype(jnp.float32)
    mean_square = jnp.mean(wide * wide, axis=-1, keepdims=True)
    normed = (wide * lax.rsqrt(mean_square + 1e-06) * gain_ref[...].reshape(1, width)).astype(jnp.bfloat16)
    scores = scores_ref[...]
    weights = 2.5 * scores / jnp.sum(scores, axis=-1, keepdims=True)
    row = lax.broadcasted_iota(jnp.int32, (tokens, 1), 0)
    live = jnp.zeros((tokens, 1), jnp.bool_)
    for request in range(requests):
        inside = (row >= request * slots) & (row <= request * slots + draft_ref[request])
        live = live | (inside & (row < (request + 1) * slots))
    weights = jnp.where(live, weights, 0.0)
    lane = lax.broadcasted_iota(jnp.int32, (tokens, extra), 1)
    coefficient = jnp.zeros((tokens, extra), jnp.float32)
    for k in range(routes_ref.shape[1]):
        coefficient += jnp.where(routes_ref[:, k : k + 1] == lane, weights[:, k : k + 1], 0.0)
    coarse = coefficient.astype(jnp.bfloat16)
    fine = (coefficient - coarse.astype(jnp.float32)).astype(jnp.bfloat16)
    out_ref[0, :, :half] = normed[:, :half]
    out_ref[1, :, :half] = normed[:, half:]
    out_ref[0, :, half:] = coarse
    out_ref[1, :, half:] = fine


def load_kernel(*refs):
    count = (len(refs) - 2) // 2
    token_ref, sems = refs[-2:]
    token_ref[...] = jnp.zeros_like(token_ref)
    copies = [
        pltpu.make_async_copy(refs[i], refs[count + i], sems.at[i]) for i in range(count)
    ]
    for copy in copies:
        copy.start()
    for copy in copies:
        copy.wait()


def spread_kernel(own_ref, other_ref, after_ref, out_ref):
    pieces = [own_ref[0], other_ref[0], own_ref[1], other_ref[1]]
    rows = jnp.concatenate([p.astype(jnp.float32) for p in pieces], axis=0).astype(jnp.bfloat16)
    for j in range(out_ref.shape[0]):
        out_ref[j] = rows


def hidden_rows(rows_ref, gate_ref, up_ref):
    half = gate_ref.shape[1] // 2
    count = rows_ref.shape[1] // 2

    def gathered(part):
        pieces = [
            rows_ref[j, part * count : (part + 1) * count, :].astype(jnp.float32)
            for j in range(rows_ref.shape[0])
        ]
        return jnp.concatenate(pieces, axis=0)

    low, high = gathered(0), gathered(1)
    mixed = low[:, half:] + high[:, half:]
    lane = lax.broadcasted_iota(jnp.int32, mixed.shape, 1)
    expert = lax.axis_index("ep") // 2
    coefficient = jnp.sum(jnp.where(lane == expert, mixed, 0.0), axis=1, keepdims=True)
    low = low[:, :half].astype(jnp.bfloat16)
    high = high[:, :half].astype(jnp.bfloat16)

    def projected(ref):
        first = jnp.dot(low, ref[0, :half], preferred_element_type=jnp.float32)
        return first + jnp.dot(high, ref[0, half:], preferred_element_type=jnp.float32)

    gate = projected(gate_ref)
    up = projected(up_ref)
    return (gate / (1.0 + jnp.exp(-gate)) * up).astype(jnp.bfloat16), coefficient


def lowered(hidden, coefficient, down_ref, out_ref, first):
    step = out_ref.shape[1] // 7
    for start in range(0, out_ref.shape[1], step):
        columns = down_ref[0, :, first + start : first + start + step]
        partial = jnp.dot(hidden, columns, preferred_element_type=jnp.float32)
        out_ref[:, start : start + step] = (partial * coefficient).astype(out_ref.dtype)


def own_kernel(rows_ref, gate_ref, up_ref, down_ref, keep_ref):
    hidden, coefficient = hidden_rows(rows_ref, gate_ref, up_ref)
    lowered(hidden, coefficient, down_ref, keep_ref, 0)


def low_kernel(
    rows_ref, gate_ref, up_ref, down_ref, after_ref, give_ref, hidden_ref, coefficient_ref
):
    hidden, coefficient = hidden_rows(rows_ref, gate_ref, up_ref)
    hidden_ref[...] = hidden
    coefficient_ref[...] = jnp.broadcast_to(coefficient, coefficient_ref.shape)
    lowered(hidden, coefficient, down_ref, give_ref, 0)


def high_kernel(hidden_ref, coefficient_ref, down_ref, give_ref):
    lowered(
        hidden_ref[...], coefficient_ref[:, :1], down_ref, give_ref, give_ref.shape[1]
    )


def fold_kernel(keep_ref, low_ref, high_ref, out_ref):
    half = keep_ref.shape[1] // 2
    count = out_ref.shape[1] // 2
    for j in range(out_ref.shape[0]):
        rows = slice(j * count, (j + 1) * count)
        low = keep_ref[rows, :half] + low_ref[rows, :].astype(jnp.float32)
        high = keep_ref[rows, half:] + high_ref[rows, :].astype(jnp.float32)
        out_ref[j] = jnp.concatenate([low, high], axis=0).astype(jnp.bfloat16)


def sum_kernel(parts_ref, keep_ref, give_ref):
    half = keep_ref.shape[1] // 2
    tokens = keep_ref.shape[0]
    total = parts_ref[0].astype(jnp.float32)
    for j in range(1, parts_ref.shape[0]):
        total += parts_ref[j].astype(jnp.float32)
    keep_ref[:, :half] = total[:tokens]
    keep_ref[:, half:] = total[2 * tokens : 3 * tokens]
    give_ref[:, :half] = total[tokens : 2 * tokens].astype(jnp.bfloat16)
    give_ref[:, half:] = total[3 * tokens :].astype(jnp.bfloat16)


def finish_kernel(keep_ref, other_ref, out_ref):
    out_ref[...] = (keep_ref[...] + other_ref[...].astype(jnp.float32)).astype(jnp.bfloat16)


def body(hidden_states, norm_gain, gate_scores, routes, draft_counts, w_gate, w_up, w_down):
    tokens, width = hidden_states.shape
    devices = lax.axis_size("ep")
    members = devices // 4
    far = devices // 2
    groups = [
        [2 * m + core + side * far for m in range(members)] for side in range(2) for core in range(2)
    ]
    half = width // 2
    carried = half + lane_round(devices // 2)
    shape = jax.ShapeDtypeStruct
    bf16, f32 = jnp.bfloat16, jnp.float32
    small = [
        pltpu.with_memory_space_constraint(a, pltpu.HBM)
        for a in (draft_counts, hidden_states, norm_gain, gate_scores, routes)
    ]
    packed = call(
        pack_kernel,
        [shape((2, tokens, carried), bf16)],
        2 * MIB,
        *small,
        specs=[HBM] * 5,
        scratch=[pltpu.SMEM(draft_counts.shape, jnp.int32)]
        + [pltpu.VMEM(a.shape, a.dtype) for a in small[1:]]
        + [pltpu.SemaphoreType.DMA((5,))],
    )
    weights = (w_gate, w_up, w_down)
    *loaded, token = call(
        load_kernel,
        [pltpu.VMEM(w.shape, w.dtype) for w in weights] + [shape((8, 128), f32)],
        MIB,
        *[pltpu.with_memory_space_constraint(w, pltpu.HBM) for w in weights],
        specs=[HBM] * 3,
        scratch=[pltpu.SemaphoreType.DMA((3,))],
    )
    loaded = [pltpu.with_memory_space_constraint(w, pltpu.VMEM) for w in loaded]
    spread = call(
        spread_kernel,
        [shape((members, 4 * tokens, carried), bf16)],
        8 * MIB,
        packed,
        swapped(packed, far),
        token,
        specs=[VMEM, VMEM, ANY],
    )

    def exchanged(array):
        return lax.all_to_all(
            array, "ep", split_axis=0, concat_axis=0, axis_index_groups=groups, tiled=True
        )

    own = exchanged(spread)
    other = swapped(own, 1)
    rows = members * 2 * tokens
    work = rows * width * w_gate.shape[2]
    keep = call(
        own_kernel,
        [shape((rows, width), f32)],
        16 * MIB,
        own,
        *loaded,
        flops=6 * work,
    )
    low, hidden, coefficient = call(
        low_kernel,
        [
            shape((rows, half), bf16),
            shape((rows, w_gate.shape[2]), bf16),
            shape((rows, 128), f32),
        ],
        16 * MIB,
        other,
        *loaded,
        keep,
        specs=[VMEM] * 4 + [ANY],
        flops=5 * work,
    )
    low = swapped(low, 1)
    high = call(
        high_kernel,
        [shape((rows, half), bf16)],
        8 * MIB,
        hidden,
        coefficient,
        loaded[2],
        flops=work,
    )
    folded = call(
        fold_kernel,
        [shape((members, 4 * tokens, half), bf16)],
        8 * MIB,
        keep,
        low,
        swapped(high, 1),
    )
    keep, give = call(
        sum_kernel,
        [shape((tokens, width), f32), shape((tokens, width), bf16)],
        8 * MIB,
        exchanged(folded),
    )
    return call(
        finish_kernel, [shape((tokens, width), bf16)], 2 * MIB, keep, swapped(give, far)
    )


def solution(mesh):
    return jax.shard_map(
        body,
        mesh=mesh,
        in_specs=(
            P(("grp", "ep"), None),
            P(),
            P(("grp", "ep"), None),
            P(("grp", "ep"), None),
            P(("grp", "ep")),
            P("ep", None, None),
            P("ep", None, None),
            P("ep", None, None),
        ),
        out_specs=P(("grp", "ep"), None),
        check_vma=False,
    )
```

```python
import math

import jax
import jax.numpy as jnp
from jax import lax
from jax.experimental import pallas as pl
from jax.experimental.pallas import tpu as pltpu
from jax.sharding import PartitionSpec as P

VMEM = pl.BlockSpec(memory_space=pltpu.VMEM)
ANY = pl.BlockSpec(memory_space=pl.ANY)
HBM = pl.BlockSpec(memory_space=pltpu.HBM)
PARTS = 4
MIB = 1024 * 1024


def swapped(array, *distances):
    size = lax.axis_size("ep")
    pairs = [(i, i ^ distances[i % len(distances)]) for i in range(size)]
    return lax.ppermute(array, "ep", pairs)


def core():
    return lax.rem(lax.axis_index("ep"), 2)


def ordered(own, other):
    first = core() == 0
    return jnp.where(first, own, other), jnp.where(first, other, own)


def wide(ref):
    return ref[...].astype(jnp.float32)


def lane_round(count):
    return -(-count // 128) * 128


def call(kernel, outs, limit, *args, specs=None, flops=0, scratch=()):
    moved = sum(math.prod(a.shape) * a.dtype.itemsize for a in (*args, *outs))
    single = len(outs) == 1
    return pl.pallas_call(
        kernel,
        out_shape=outs[0] if single else tuple(outs),
        in_specs=specs or [VMEM] * len(args),
        out_specs=VMEM if single else tuple([VMEM] * len(outs)),
        scratch_shapes=list(scratch),
        compiler_params=pltpu.CompilerParams(vmem_limit_bytes=limit),
        cost_estimate=pl.CostEstimate(flops=flops, bytes_accessed=moved, transcendentals=0),
    )(*args)


def pack_kernel(
    draft_hbm, states_hbm, gain_hbm, scores_hbm, routes_hbm, out_ref,
    draft_ref, states_ref, gain_ref, scores_ref, routes_ref, sems,
):
    sources = (draft_hbm, states_hbm, gain_hbm, scores_hbm, routes_hbm)
    targets = (draft_ref, states_ref, gain_ref, scores_ref, routes_ref)
    copies = [
        pltpu.make_async_copy(source, target, sems.at[i])
        for i, (source, target) in enumerate(zip(sources, targets))
    ]
    for copy in copies:
        copy.start()
    for copy in copies:
        copy.wait()
    tokens, width = states_ref.shape
    piece = width // PARTS
    extra = out_ref.shape[1] - piece
    requests = draft_ref.shape[0]
    slots = tokens // requests
    states = wide(states_ref)
    mean_square = jnp.mean(states * states, axis=-1, keepdims=True)
    normed = (states * lax.rsqrt(mean_square + 1e-06) * gain_ref[...].reshape(1, width)).astype(jnp.bfloat16)
    scores = scores_ref[...]
    weights = 2.5 * scores / jnp.sum(scores, axis=-1, keepdims=True)
    row = lax.broadcasted_iota(jnp.int32, (tokens, 1), 0)
    live = jnp.zeros((tokens, 1), jnp.bool_)
    for request in range(requests):
        inside = (row >= request * slots) & (row <= request * slots + draft_ref[request])
        live = live | (inside & (row < (request + 1) * slots))
    weights = jnp.where(live, weights, 0.0)
    lane = lax.broadcasted_iota(jnp.int32, (tokens, extra), 1)
    coefficient = jnp.zeros((tokens, extra), jnp.float32)
    for k in range(routes_ref.shape[1]):
        coefficient += jnp.where(routes_ref[:, k : k + 1] == lane, weights[:, k : k + 1], 0.0)
    coarse = coefficient.astype(jnp.bfloat16)
    fine = (coefficient - coarse.astype(jnp.float32)).astype(jnp.bfloat16)
    zero = jnp.zeros((tokens, extra), jnp.float32)
    coarse, fine = coarse.astype(jnp.float32), fine.astype(jnp.float32)
    sides = [coarse, fine] + [zero] * (PARTS - 2)
    normed = normed.astype(jnp.float32)
    normed = jnp.concatenate([normed[:, p * piece : (p + 1) * piece] for p in range(PARTS)], axis=0)
    rows = jnp.concatenate([normed, jnp.concatenate(sides, axis=0)], axis=1).astype(jnp.bfloat16)
    out_ref[...] = rows


def load_kernel(*refs):
    count = (len(refs) - 2) // 2
    token_ref, sems = refs[-2:]
    token_ref[...] = jnp.zeros_like(token_ref)
    copies = [
        pltpu.make_async_copy(refs[i], refs[count + i], sems.at[i]) for i in range(count)
    ]
    for copy in copies:
        copy.start()
    for copy in copies:
        copy.wait()


def combine_kernel(own_ref, beside_ref, far_ref, far_beside_ref, after_ref, out_ref, side_ref):
    tokens = own_ref.shape[0] // PARTS
    piece = own_ref.shape[1] - (PARTS * own_ref.shape[1] - out_ref.shape[1]) // 2

    def unfolded(rows):
        parts = [rows[p * tokens : (p + 1) * tokens] for p in range(PARTS)]
        columns = []
        for side in range(2):
            columns += [p[:, :piece] for p in parts[2 * side : 2 * side + 2]]
            columns.append(parts[side][:, piece:])
        return jnp.concatenate(columns, axis=1)

    blocks = ordered(wide(own_ref), wide(beside_ref)) + ordered(wide(far_ref), wide(far_beside_ref))
    rows = jnp.concatenate([unfolded(b) for b in blocks], axis=0)
    out_ref[...] = rows.astype(jnp.bfloat16)
    middle = rows.shape[1] // 2
    side_ref[...] = ordered(rows[:, :middle], rows[:, middle:])[0].astype(jnp.bfloat16)


def hidden_rows(lows, highs, gate_ref, up_ref):
    half = gate_ref.shape[1] // 2
    low, high = jnp.concatenate(lows, axis=0), jnp.concatenate(highs, axis=0)
    mixed = low[:, half:] + high[:, half:]
    lane = lax.broadcasted_iota(jnp.int32, mixed.shape, 1)
    expert = lax.axis_index("ep") // 2
    coefficient = jnp.sum(jnp.where(lane == expert, mixed, 0.0), axis=1, keepdims=True)
    low = low[:, :half].astype(jnp.bfloat16)
    high = high[:, :half].astype(jnp.bfloat16)

    def projected(ref):
        first = jnp.dot(low, ref[0, :half], preferred_element_type=jnp.float32)
        return first + jnp.dot(high, ref[0, half:], preferred_element_type=jnp.float32)

    gate = projected(gate_ref)
    up = projected(up_ref)
    return (gate / (1.0 + jnp.exp(-gate)) * up).astype(jnp.bfloat16), coefficient


def halves(ref):
    middle = ref.shape[1] // 2
    return ref[:, :middle].astype(jnp.float32), ref[:, middle:].astype(jnp.float32)


def lowered(hidden, coefficient, down_ref, first, count):
    columns = down_ref[0, :, first : first + count]
    return jnp.dot(hidden, columns, preferred_element_type=jnp.float32) * coefficient


def own_kernel(*refs):
    *refs, keep_ref, side_keep_ref, side_give_ref, down_ref, sem = refs
    block_ref, side_ref, side_beside_ref, *others, gate_ref, up_ref, down_hbm = refs
    copy = pltpu.make_async_copy(down_hbm, down_ref, sem)
    copy.start()
    lows, highs = zip(*[halves(ref) for ref in (block_ref, *others)])
    side_low, side_high = ordered(wide(side_ref), wide(side_beside_ref))
    hidden, coefficient = hidden_rows(
        [*lows, side_low], [*highs, side_high], gate_ref, up_ref
    )
    copy.wait()
    rows, width = keep_ref.shape
    half = width // 2
    step = half // 2
    for start in range(0, half, step):
        low = lowered(hidden, coefficient, down_ref, start, step)
        high = lowered(hidden, coefficient, down_ref, half + start, step)
        keep_ref[:, start : start + step] = low[:rows]
        keep_ref[:, half + start : half + start + step] = high[:rows]
        keep, give = ordered(low[rows:], high[rows:])
        side_keep_ref[:, start : start + step] = keep
        side_give_ref[:, start : start + step] = give.astype(jnp.bfloat16)


def low_kernel(*refs):
    *others, gate_ref, up_ref, down_ref, after_ref, give_ref, hidden_ref, coefficient_ref = refs
    lows, highs = zip(*[halves(ref) for ref in others])
    hidden, coefficient = hidden_rows(lows, highs, gate_ref, up_ref)
    hidden_ref[...] = hidden
    coefficient_ref[...] = jnp.broadcast_to(coefficient, coefficient_ref.shape)
    half = give_ref.shape[1]
    step = half // 2
    for start in range(0, half, step):
        low = lowered(hidden, coefficient, down_ref, start, step)
        give_ref[:, start : start + step] = low.astype(jnp.bfloat16)


def high_kernel(hidden_ref, coefficient_ref, down_ref, give_ref):
    hidden, coefficient = hidden_ref[...], coefficient_ref[:, :1]
    half = give_ref.shape[1]
    step = half // 2
    for start in range(0, half, step):
        high = lowered(hidden, coefficient, down_ref, half + start, step)
        give_ref[:, start : start + step] = high.astype(jnp.bfloat16)


def fold_kernel(*refs):
    keep_ref, low_ref, high_ref, side_keep_ref, side_other_ref, *outs, side_out_ref = refs
    half = low_ref.shape[1]
    count = side_out_ref.shape[0]
    side_out_ref[...] = (side_keep_ref[...] + wide(side_other_ref)).astype(jnp.bfloat16)
    for j, out_ref in enumerate(outs):
        rows = slice(j * count, (j + 1) * count)
        kept = slice((j + 1) * count, (j + 2) * count)
        low = keep_ref[kept, :half] + low_ref[rows, :].astype(jnp.float32)
        high = keep_ref[kept, half:] + high_ref[rows, :].astype(jnp.float32)
        out_ref[:, :half] = low.astype(jnp.bfloat16)
        out_ref[:, half:] = high.astype(jnp.bfloat16)


def sum_kernel(*refs):
    keep_ref, side_ref, *parts, mine_ref, give_ref = refs
    rows, half = side_ref.shape
    tokens = rows // 4
    total = keep_ref[:rows, :]
    for ref in parts:
        total += wide(ref)
    side = wide(side_ref)
    zero = jnp.zeros_like(side)
    total += jnp.concatenate(ordered(side, zero), axis=1)
    near = ordered(total[:tokens], total[tokens : 2 * tokens])
    far = ordered(total[2 * tokens : 3 * tokens], total[3 * tokens :])

    def folded(which):
        columns = (slice(0, half), slice(half, 2 * half))
        return jnp.concatenate([b[which][:, c] for c in columns for b in (near, far)], axis=0)

    mine_ref[...] = folded(0)
    give_ref[...] = folded(1).astype(jnp.bfloat16)


def split_kernel(mine_ref, other_ref, near_ref, far_ref):
    total = mine_ref[...] + wide(other_ref)
    tokens = total.shape[0] // 4
    piece = near_ref.shape[1]

    def folded(which):
        pieces = []
        for side in range(2):
            start = (2 * side + which) * tokens
            rows = total[start : start + tokens]
            pieces += [rows[:, :piece], rows[:, piece:]]
        return jnp.concatenate(pieces, axis=0)

    near_ref[...] = folded(0)
    far_ref[...] = folded(1).astype(jnp.bfloat16)


def finish_kernel(near_ref, other_ref, out_ref):
    tokens, width = out_ref.shape
    piece = width // PARTS
    total = near_ref[...] + wide(other_ref)
    for p in range(PARTS):
        rows = total[p * tokens : (p + 1) * tokens]
        out_ref[:, p * piece : (p + 1) * piece] = rows.astype(jnp.bfloat16)


def body(hidden_states, norm_gain, gate_scores, routes, draft_counts, w_gate, w_up, w_down):
    tokens, width = hidden_states.shape
    devices = lax.axis_size("ep")
    far = devices // 2
    hops = sorted(range(2, far, 2), key=lambda hop: hop.bit_count())
    shared, others = hops[0], hops[1:]
    steps = [(others[i], others[i + 1]) for i in range(0, len(others), 2)][::-1]
    half, piece = width // 2, width // PARTS
    extra = lane_round(far)
    shape = jax.ShapeDtypeStruct
    bf16, f32 = jnp.bfloat16, jnp.float32
    inner = w_gate.shape[2]

    small = [
        pltpu.with_memory_space_constraint(a, pltpu.HBM)
        for a in (draft_counts, hidden_states, norm_gain, gate_scores, routes)
    ]
    packed = call(
        pack_kernel,
        [shape((PARTS * tokens, piece + extra), bf16)],
        4 * MIB,
        *small,
        specs=[HBM] * 5,
        scratch=[pltpu.SMEM(draft_counts.shape, jnp.int32)]
        + [pltpu.VMEM(a.shape, a.dtype) for a in small[1:]]
        + [pltpu.SemaphoreType.DMA((5,))],
    )
    moved = swapped(packed, far)
    beside = swapped(packed, 1)
    weights = [pltpu.with_memory_space_constraint(w, pltpu.HBM) for w in (w_gate, w_up, w_down)]
    gate, up, token = call(
        load_kernel,
        [pltpu.VMEM(w.shape, w.dtype) for w in weights[:2]] + [shape((8, 128), f32)],
        MIB,
        *weights[:2],
        specs=[HBM] * 2,
        scratch=[pltpu.SemaphoreType.DMA((2,))],
    )
    gate, up = [pltpu.with_memory_space_constraint(w, pltpu.VMEM) for w in (gate, up)]
    rows = 4 * tokens
    block, side = call(
        combine_kernel,
        [shape((rows, width + 2 * extra), bf16), shape((rows, half + extra), bf16)],
        4 * MIB,
        packed,
        beside,
        moved,
        swapped(moved, 1),
        token,
        specs=[VMEM] * 4 + [ANY],
    )
    side = swapped(side, shared)
    parts = [swapped(block, *step) for step in steps]
    side_beside = swapped(side, 1)
    beside = [swapped(part, 1) for part in parts]
    count = len(steps)
    work = 2 * rows * width * inner
    keep, side_keep, side_give, down = call(
        own_kernel,
        [
            shape(((1 + count) * rows, width), f32),
            shape((rows, half), f32),
            shape((rows, half), bf16),
            pltpu.VMEM(w_down.shape, w_down.dtype),
        ],
        16 * MIB,
        block,
        side,
        side_beside,
        *parts,
        gate,
        up,
        weights[2],
        specs=[VMEM] * (5 + count) + [HBM],
        flops=3 * (2 + count) * work,
        scratch=[pltpu.SemaphoreType.DMA],
    )
    down = pltpu.with_memory_space_constraint(down, pltpu.VMEM)
    side_give = swapped(side_give, 1)
    low, hidden, coefficient = call(
        low_kernel,
        [
            shape((count * rows, half), bf16),
            shape((count * rows, inner), bf16),
            shape((count * rows, 128), f32),
        ],
        16 * MIB,
        *beside,
        gate,
        up,
        down,
        keep,
        specs=[VMEM] * (3 + count) + [ANY],
        flops=5 * count * work // 2,
    )
    low = swapped(low, 1)
    high = call(
        high_kernel,
        [shape((count * rows, half), bf16)],
        8 * MIB,
        hidden,
        coefficient,
        down,
        flops=count * work // 2,
    )
    high = swapped(high, 1)
    *parts, side = call(
        fold_kernel,
        [shape((rows, width), bf16)] * count + [shape((rows, half), bf16)],
        8 * MIB,
        keep,
        low,
        high,
        side_keep,
        side_give,
    )
    side = swapped(side, shared)
    parts = [swapped(part, *step) for part, step in zip(parts, steps)]
    mine, give = call(
        sum_kernel,
        [shape((rows, half), f32), shape((rows, half), bf16)],
        8 * MIB,
        keep,
        side,
        *parts,
    )
    near, give = call(
        split_kernel,
        [shape((PARTS * tokens, piece), f32), shape((PARTS * tokens, piece), bf16)],
        4 * MIB,
        mine,
        swapped(give, 1),
    )
    return call(
        finish_kernel, [shape((tokens, width), bf16)], 4 * MIB, near, swapped(give, far)
    )


def solution(mesh):
    return jax.shard_map(
        body,
        mesh=mesh,
        in_specs=(
            P(("grp", "ep"), None),
            P(),
            P(("grp", "ep"), None),
            P(("grp", "ep"), None),
            P(("grp", "ep")),
            P("ep", None, None),
            P("ep", None, None),
            P("ep", None, None),
        ),
        out_specs=P(("grp", "ep"), None),
        check_vma=False,
    )
```

```python
import math

import jax
import jax.numpy as jnp
from jax import lax
from jax.experimental import pallas as pl
from jax.experimental.pallas import tpu as pltpu
from jax.sharding import PartitionSpec as P


VMEM = pl.BlockSpec(memory_space=pltpu.VMEM)
ANY = pl.BlockSpec(memory_space=pl.ANY)
HBM = pl.BlockSpec(memory_space=pltpu.HBM)
PARTS = 4
MIB = 1024 * 1024


def swapped(array, *distances):
    size = lax.axis_size("ep")
    pairs = [(i, i ^ distances[i % len(distances)]) for i in range(size)]
    return lax.ppermute(array, "ep", pairs)


def core():
    return lax.rem(lax.axis_index("ep"), 2)


def ordered(own, other):
    first = core() == 0
    return jnp.where(first, own, other), jnp.where(first, other, own)


def wide(ref):
    return ref[...].astype(jnp.float32)


def lane_round(count):
    return -(-count // 128) * 128


def call(kernel, outs, limit, *args, specs=None, flops=0, scratch=()):
    moved = sum(math.prod(a.shape) * a.dtype.itemsize for a in (*args, *outs))
    single = len(outs) == 1
    return pl.pallas_call(
        kernel,
        out_shape=outs[0] if single else tuple(outs),
        in_specs=specs or [VMEM] * len(args),
        out_specs=VMEM if single else tuple([VMEM] * len(outs)),
        scratch_shapes=list(scratch),
        compiler_params=pltpu.CompilerParams(vmem_limit_bytes=limit),
        cost_estimate=pl.CostEstimate(flops=flops, bytes_accessed=moved, transcendentals=0),
    )(*args)


def pack_kernel(
    draft_hbm, states_hbm, gain_hbm, scores_hbm, routes_hbm, out_ref,
    draft_ref, states_ref, gain_ref, scores_ref, routes_ref, sems,
):
    sources = (draft_hbm, states_hbm, gain_hbm, scores_hbm, routes_hbm)
    targets = (draft_ref, states_ref, gain_ref, scores_ref, routes_ref)
    copies = [
        pltpu.make_async_copy(source, target, sems.at[i])
        for i, (source, target) in enumerate(zip(sources, targets))
    ]
    for copy in copies:
        copy.start()
    for copy in copies:
        copy.wait()
    tokens, width = states_ref.shape
    piece = width // PARTS
    extra = out_ref.shape[1] - piece
    requests = draft_ref.shape[0]
    slots = tokens // requests
    states = wide(states_ref)
    mean_square = jnp.mean(states * states, axis=-1, keepdims=True)
    normed = (states * lax.rsqrt(mean_square + 1e-06) * gain_ref[...].reshape(1, width)).astype(jnp.bfloat16)
    scores = scores_ref[...]
    weights = 2.5 * scores / jnp.sum(scores, axis=-1, keepdims=True)
    row = lax.broadcasted_iota(jnp.int32, (tokens, 1), 0)
    live = jnp.zeros((tokens, 1), jnp.bool_)
    for request in range(requests):
        inside = (row >= request * slots) & (row <= request * slots + draft_ref[request])
        live = live | (inside & (row < (request + 1) * slots))
    weights = jnp.where(live, weights, 0.0)
    lane = lax.broadcasted_iota(jnp.int32, (tokens, extra), 1)
    coefficient = jnp.zeros((tokens, extra), jnp.float32)
    for k in range(routes_ref.shape[1]):
        coefficient += jnp.where(routes_ref[:, k : k + 1] == lane, weights[:, k : k + 1], 0.0)
    coarse = coefficient.astype(jnp.bfloat16)
    fine = (coefficient - coarse.astype(jnp.float32)).astype(jnp.bfloat16)
    zero = jnp.zeros((tokens, extra), jnp.float32)
    coarse, fine = coarse.astype(jnp.float32), fine.astype(jnp.float32)
    sides = [coarse, fine] + [zero] * (PARTS - 2)
    normed = normed.astype(jnp.float32)
    normed = jnp.concatenate([normed[:, p * piece : (p + 1) * piece] for p in range(PARTS)], axis=0)
    rows = jnp.concatenate([normed, jnp.concatenate(sides, axis=0)], axis=1).astype(jnp.bfloat16)
    out_ref[...] = rows


def load_kernel(*refs):
    count = (len(refs) - 2) // 2
    token_ref, sems = refs[-2:]
    token_ref[...] = jnp.zeros_like(token_ref)
    copies = [
        pltpu.make_async_copy(refs[i], refs[count + i], sems.at[i]) for i in range(count)
    ]
    for copy in copies:
        copy.start()
    for copy in copies:
        copy.wait()


def combine_kernel(own_ref, beside_ref, far_ref, far_beside_ref, after_ref, out_ref, side_ref):
    tokens = own_ref.shape[0] // PARTS
    piece = own_ref.shape[1] - (PARTS * own_ref.shape[1] - out_ref.shape[1]) // 2

    def unfolded(rows):
        parts = [rows[p * tokens : (p + 1) * tokens] for p in range(PARTS)]
        columns = []
        for side in range(2):
            columns += [p[:, :piece] for p in parts[2 * side : 2 * side + 2]]
            columns.append(parts[side][:, piece:])
        return jnp.concatenate(columns, axis=1)

    blocks = ordered(wide(own_ref), wide(beside_ref)) + ordered(wide(far_ref), wide(far_beside_ref))
    rows = jnp.concatenate([unfolded(b) for b in blocks], axis=0)
    out_ref[...] = rows.astype(jnp.bfloat16)
    middle = rows.shape[1] // 2
    side_ref[...] = ordered(rows[:, :middle], rows[:, middle:])[0].astype(jnp.bfloat16)


def hidden_rows(lows, highs, gate_ref, up_ref):
    half = gate_ref.shape[1] // 2
    low, high = jnp.concatenate(lows, axis=0), jnp.concatenate(highs, axis=0)
    mixed = low[:, half:] + high[:, half:]
    lane = lax.broadcasted_iota(jnp.int32, mixed.shape, 1)
    expert = lax.axis_index("ep") // 2
    coefficient = jnp.sum(jnp.where(lane == expert, mixed, 0.0), axis=1, keepdims=True)
    low = low[:, :half].astype(jnp.bfloat16)
    high = high[:, :half].astype(jnp.bfloat16)

    def projected(ref):
        first = jnp.dot(low, ref[0, :half], preferred_element_type=jnp.float32)
        return first + jnp.dot(high, ref[0, half:], preferred_element_type=jnp.float32)

    gate = projected(gate_ref)
    up = projected(up_ref)
    return (gate / (1.0 + jnp.exp(-gate)) * up).astype(jnp.bfloat16), coefficient


def halves(ref):
    middle = ref.shape[1] // 2
    return ref[:, :middle].astype(jnp.float32), ref[:, middle:].astype(jnp.float32)


def lowered(hidden, coefficient, down_ref, first, count):
    columns = down_ref[0, :, first : first + count]
    return jnp.dot(hidden, columns, preferred_element_type=jnp.float32) * coefficient


def own_kernel(*refs):
    *refs, keep_ref, side_keep_ref, side_give_ref = refs
    block_ref, side_ref, side_beside_ref, *others, gate_ref, up_ref, down_ref = refs
    lows, highs = zip(*[halves(ref) for ref in (block_ref, *others)])
    side_low, side_high = ordered(wide(side_ref), wide(side_beside_ref))
    hidden, coefficient = hidden_rows(
        [*lows, side_low], [*highs, side_high], gate_ref, up_ref
    )
    rows, width = keep_ref.shape
    half = width // 2
    step = half // 2
    for start in range(0, half, step):
        low = lowered(hidden, coefficient, down_ref, start, step)
        high = lowered(hidden, coefficient, down_ref, half + start, step)
        keep_ref[:, start : start + step] = low[:rows]
        keep_ref[:, half + start : half + start + step] = high[:rows]
        keep, give = ordered(low[rows:], high[rows:])
        side_keep_ref[:, start : start + step] = keep
        side_give_ref[:, start : start + step] = give.astype(jnp.bfloat16)


def low_kernel(*refs):
    *others, gate_ref, up_ref, down_ref, after_ref, give_ref, hidden_ref, coefficient_ref = refs
    lows, highs = zip(*[halves(ref) for ref in others])
    hidden, coefficient = hidden_rows(lows, highs, gate_ref, up_ref)
    hidden_ref[...] = hidden
    coefficient_ref[...] = jnp.broadcast_to(coefficient, coefficient_ref.shape)
    half = give_ref.shape[1]
    step = half // 2
    for start in range(0, half, step):
        low = lowered(hidden, coefficient, down_ref, start, step)
        give_ref[:, start : start + step] = low.astype(jnp.bfloat16)


def high_kernel(hidden_ref, coefficient_ref, down_ref, give_ref):
    hidden, coefficient = hidden_ref[...], coefficient_ref[:, :1]
    half = give_ref.shape[1]
    step = half // 2
    for start in range(0, half, step):
        high = lowered(hidden, coefficient, down_ref, half + start, step)
        give_ref[:, start : start + step] = high.astype(jnp.bfloat16)


def fold_kernel(*refs):
    keep_ref, low_ref, high_ref, side_keep_ref, side_other_ref, *outs, side_out_ref = refs
    half = low_ref.shape[1]
    count = side_out_ref.shape[0]
    side_out_ref[...] = (side_keep_ref[...] + wide(side_other_ref)).astype(jnp.bfloat16)
    for j, out_ref in enumerate(outs):
        rows = slice(j * count, (j + 1) * count)
        kept = slice((j + 1) * count, (j + 2) * count)
        low = keep_ref[kept, :half] + low_ref[rows, :].astype(jnp.float32)
        high = keep_ref[kept, half:] + high_ref[rows, :].astype(jnp.float32)
        out_ref[:, :half] = low.astype(jnp.bfloat16)
        out_ref[:, half:] = high.astype(jnp.bfloat16)


def sum_kernel(*refs):
    keep_ref, side_ref, *parts, mine_ref, give_ref = refs
    rows, half = side_ref.shape
    tokens = rows // 4
    total = keep_ref[:rows, :]
    for ref in parts:
        total += wide(ref)
    side = wide(side_ref)
    zero = jnp.zeros_like(side)
    total += jnp.concatenate(ordered(side, zero), axis=1)
    near = ordered(total[:tokens], total[tokens : 2 * tokens])
    far = ordered(total[2 * tokens : 3 * tokens], total[3 * tokens :])

    def folded(which):
        columns = (slice(0, half), slice(half, 2 * half))
        return jnp.concatenate([b[which][:, c] for c in columns for b in (near, far)], axis=0)

    mine_ref[...] = folded(0)
    give_ref[...] = folded(1).astype(jnp.bfloat16)


def split_kernel(mine_ref, other_ref, near_ref, far_ref):
    total = mine_ref[...] + wide(other_ref)
    tokens = total.shape[0] // 4
    piece = near_ref.shape[1]

    def folded(which):
        pieces = []
        for side in range(2):
            start = (2 * side + which) * tokens
            rows = total[start : start + tokens]
            pieces += [rows[:, :piece], rows[:, piece:]]
        return jnp.concatenate(pieces, axis=0)

    near_ref[...] = folded(0)
    far_ref[...] = folded(1).astype(jnp.bfloat16)


def finish_kernel(near_ref, other_ref, out_ref):
    tokens, width = out_ref.shape
    piece = width // PARTS
    total = near_ref[...] + wide(other_ref)
    for p in range(PARTS):
        rows = total[p * tokens : (p + 1) * tokens]
        out_ref[:, p * piece : (p + 1) * piece] = rows.astype(jnp.bfloat16)


def body(hidden_states, norm_gain, gate_scores, routes, draft_counts, w_gate, w_up, w_down):
    tokens, width = hidden_states.shape
    devices = lax.axis_size("ep")
    far = devices // 2
    shared = far - 2
    steps = [(hop, shared ^ hop) for hop in range(2, far // 2, 2)]
    half, piece = width // 2, width // PARTS
    extra = lane_round(far)
    shape = jax.ShapeDtypeStruct
    bf16, f32 = jnp.bfloat16, jnp.float32
    inner = w_gate.shape[2]

    small = [
        pltpu.with_memory_space_constraint(a, pltpu.HBM)
        for a in (draft_counts, hidden_states, norm_gain, gate_scores, routes)
    ]
    packed = call(
        pack_kernel,
        [shape((PARTS * tokens, piece + extra), bf16)],
        4 * MIB,
        *small,
        specs=[HBM] * 5,
        scratch=[pltpu.SMEM(draft_counts.shape, jnp.int32)]
        + [pltpu.VMEM(a.shape, a.dtype) for a in small[1:]]
        + [pltpu.SemaphoreType.DMA((5,))],
    )
    moved = swapped(packed, far)
    beside = swapped(packed, 1)
    weights = [pltpu.with_memory_space_constraint(w, pltpu.HBM) for w in (w_gate, w_up, w_down)]
    gate, up, token = call(
        load_kernel,
        [pltpu.VMEM(w.shape, w.dtype) for w in weights[:2]] + [shape((8, 128), f32)],
        MIB,
        *weights[:2],
        specs=[HBM] * 2,
        scratch=[pltpu.SemaphoreType.DMA((2,))],
    )
    gate, up = [pltpu.with_memory_space_constraint(w, pltpu.VMEM) for w in (gate, up)]
    rows = 4 * tokens
    block, side = call(
        combine_kernel,
        [shape((rows, width + 2 * extra), bf16), shape((rows, half + extra), bf16)],
        4 * MIB,
        packed,
        beside,
        moved,
        swapped(moved, 1),
        token,
        specs=[VMEM] * 4 + [ANY],
    )
    side = swapped(side, shared)
    parts = [swapped(block, *step) for step in steps]
    side_beside = swapped(side, 1)
    beside = [swapped(part, 1) for part in parts]
    count = len(steps)
    work = 2 * rows * width * inner
    down, token = call(
        load_kernel,
        [pltpu.VMEM(w_down.shape, w_down.dtype), shape((8, 128), f32)],
        MIB,
        weights[2],
        specs=[HBM],
        scratch=[pltpu.SemaphoreType.DMA((1,))],
    )
    down = pltpu.with_memory_space_constraint(down, pltpu.VMEM)
    keep, side_keep, side_give = call(
        own_kernel,
        [
            shape(((1 + count) * rows, width), f32),
            shape((rows, half), f32),
            shape((rows, half), bf16),
        ],
        16 * MIB,
        block,
        side,
        side_beside,
        *parts,
        gate,
        up,
        down,
        flops=3 * (2 + count) * work,
    )
    side_give = swapped(side_give, 1)
    low, hidden, coefficient = call(
        low_kernel,
        [
            shape((count * rows, half), bf16),
            shape((count * rows, inner), bf16),
            shape((count * rows, 128), f32),
        ],
        16 * MIB,
        *beside,
        gate,
        up,
        down,
        keep,
        specs=[VMEM] * (3 + count) + [ANY],
        flops=5 * count * work // 2,
    )
    low = swapped(low, 1)
    high = call(
        high_kernel,
        [shape((count * rows, half), bf16)],
        8 * MIB,
        hidden,
        coefficient,
        down,
        flops=count * work // 2,
    )
    high = swapped(high, 1)
    *parts, side = call(
        fold_kernel,
        [shape((rows, width), bf16)] * count + [shape((rows, half), bf16)],
        8 * MIB,
        keep,
        low,
        high,
        side_keep,
        side_give,
    )
    side = swapped(side, shared)
    parts = [swapped(part, *step) for part, step in zip(parts, steps)]
    mine, give = call(
        sum_kernel,
        [shape((rows, half), f32), shape((rows, half), bf16)],
        8 * MIB,
        keep,
        side,
        *parts,
    )
    near, give = call(
        split_kernel,
        [shape((PARTS * tokens, piece), f32), shape((PARTS * tokens, piece), bf16)],
        4 * MIB,
        mine,
        swapped(give, 1),
    )
    return call(finish_kernel, [shape((tokens, width), bf16)], 4 * MIB, near, swapped(give, far))


def solution(mesh):
    return jax.shard_map(
        body,
        mesh=mesh,
        in_specs=(
            P(("grp", "ep"), None),
            P(),
            P(("grp", "ep"), None),
            P(("grp", "ep"), None),
            P(("grp", "ep")),
            P("ep", None, None),
            P("ep", None, None),
            P("ep", None, None),
        ),
        out_specs=P(("grp", "ep"), None),
        check_vma=False,
    )
```

```python
import math

import jax
import jax.numpy as jnp
from jax import lax
from jax.experimental import pallas as pl
from jax.experimental.pallas import tpu as pltpu
from jax.sharding import PartitionSpec as P


VMEM = pl.BlockSpec(memory_space=pltpu.VMEM)
ANY = pl.BlockSpec(memory_space=pl.ANY)
HBM = pl.BlockSpec(memory_space=pltpu.HBM)
PARTS = 4
MIB = 1024 * 1024


def swapped(array, *distances):
    size = lax.axis_size("ep")
    pairs = [(i, i ^ distances[i % len(distances)]) for i in range(size)]
    return lax.ppermute(array, "ep", pairs)


def core():
    return lax.rem(lax.axis_index("ep"), 2)


def ordered(own, other):
    first = core() == 0
    return jnp.where(first, own, other), jnp.where(first, other, own)


def wide(ref):
    return ref[...].astype(jnp.float32)


def lane_round(count):
    return -(-count // 128) * 128


def call(kernel, outs, limit, *args, specs=None, flops=0, scratch=()):
    moved = sum(math.prod(a.shape) * a.dtype.itemsize for a in (*args, *outs))
    single = len(outs) == 1
    return pl.pallas_call(
        kernel,
        out_shape=outs[0] if single else tuple(outs),
        in_specs=specs or [VMEM] * len(args),
        out_specs=VMEM if single else tuple([VMEM] * len(outs)),
        scratch_shapes=list(scratch),
        compiler_params=pltpu.CompilerParams(vmem_limit_bytes=limit),
        cost_estimate=pl.CostEstimate(flops=flops, bytes_accessed=moved, transcendentals=0),
    )(*args)


def pack_kernel(
    draft_hbm, states_hbm, gain_hbm, scores_hbm, routes_hbm, out_ref,
    draft_ref, states_ref, gain_ref, scores_ref, routes_ref, sems,
):
    sources = (draft_hbm, states_hbm, gain_hbm, scores_hbm, routes_hbm)
    targets = (draft_ref, states_ref, gain_ref, scores_ref, routes_ref)
    copies = [
        pltpu.make_async_copy(source, target, sems.at[i])
        for i, (source, target) in enumerate(zip(sources, targets))
    ]
    for copy in copies:
        copy.start()
    for copy in copies:
        copy.wait()
    tokens, width = states_ref.shape
    piece = width // PARTS
    extra = out_ref.shape[1] - piece
    requests = draft_ref.shape[0]
    slots = tokens // requests
    states = wide(states_ref)
    mean_square = jnp.mean(states * states, axis=-1, keepdims=True)
    normed = (states * lax.rsqrt(mean_square + 1e-06) * gain_ref[...].reshape(1, width)).astype(jnp.bfloat16)
    scores = scores_ref[...]
    weights = 2.5 * scores / jnp.sum(scores, axis=-1, keepdims=True)
    row = lax.broadcasted_iota(jnp.int32, (tokens, 1), 0)
    live = jnp.zeros((tokens, 1), jnp.bool_)
    for request in range(requests):
        inside = (row >= request * slots) & (row <= request * slots + draft_ref[request])
        live = live | (inside & (row < (request + 1) * slots))
    weights = jnp.where(live, weights, 0.0)
    lane = lax.broadcasted_iota(jnp.int32, (tokens, extra), 1)
    coefficient = jnp.zeros((tokens, extra), jnp.float32)
    for k in range(routes_ref.shape[1]):
        coefficient += jnp.where(routes_ref[:, k : k + 1] == lane, weights[:, k : k + 1], 0.0)
    coarse = coefficient.astype(jnp.bfloat16)
    fine = (coefficient - coarse.astype(jnp.float32)).astype(jnp.bfloat16)
    zero = jnp.zeros((tokens, extra), jnp.float32)
    coarse, fine = coarse.astype(jnp.float32), fine.astype(jnp.float32)
    sides = [coarse, fine] + [zero] * (PARTS - 2)
    normed = normed.astype(jnp.float32)
    normed = jnp.concatenate([normed[:, p * piece : (p + 1) * piece] for p in range(PARTS)], axis=0)
    rows = jnp.concatenate([normed, jnp.concatenate(sides, axis=0)], axis=1).astype(jnp.bfloat16)
    out_ref[...] = rows


def load_kernel(*refs):
    count = (len(refs) - 2) // 2
    token_ref, sems = refs[-2:]
    token_ref[...] = jnp.zeros_like(token_ref)
    copies = [
        pltpu.make_async_copy(refs[i], refs[count + i], sems.at[i]) for i in range(count)
    ]
    for copy in copies:
        copy.start()
    for copy in copies:
        copy.wait()


def combine_kernel(own_ref, beside_ref, far_ref, far_beside_ref, after_ref, out_ref, side_ref):
    tokens = own_ref.shape[0] // PARTS
    piece = own_ref.shape[1] - (PARTS * own_ref.shape[1] - out_ref.shape[1]) // 2

    def unfolded(rows):
        parts = [rows[p * tokens : (p + 1) * tokens] for p in range(PARTS)]
        columns = []
        for side in range(2):
            columns += [p[:, :piece] for p in parts[2 * side : 2 * side + 2]]
            columns.append(parts[side][:, piece:])
        return jnp.concatenate(columns, axis=1)

    blocks = ordered(wide(own_ref), wide(beside_ref)) + ordered(wide(far_ref), wide(far_beside_ref))
    rows = jnp.concatenate([unfolded(b) for b in blocks], axis=0)
    out_ref[...] = rows.astype(jnp.bfloat16)
    middle = rows.shape[1] // 2
    side_ref[...] = ordered(rows[:, :middle], rows[:, middle:])[0].astype(jnp.bfloat16)


def hidden_rows(lows, highs, gate_ref, up_ref):
    half = gate_ref.shape[1] // 2
    low, high = jnp.concatenate(lows, axis=0), jnp.concatenate(highs, axis=0)
    mixed = low[:, half:] + high[:, half:]
    lane = lax.broadcasted_iota(jnp.int32, mixed.shape, 1)
    expert = lax.axis_index("ep") // 2
    coefficient = jnp.sum(jnp.where(lane == expert, mixed, 0.0), axis=1, keepdims=True)
    low = low[:, :half].astype(jnp.bfloat16)
    high = high[:, :half].astype(jnp.bfloat16)

    def projected(ref):
        first = jnp.dot(low, ref[0, :half], preferred_element_type=jnp.float32)
        return first + jnp.dot(high, ref[0, half:], preferred_element_type=jnp.float32)

    gate = projected(gate_ref)
    up = projected(up_ref)
    return (gate / (1.0 + jnp.exp(-gate)) * up).astype(jnp.bfloat16), coefficient


def halves(ref):
    middle = ref.shape[1] // 2
    return ref[:, :middle].astype(jnp.float32), ref[:, middle:].astype(jnp.float32)


def lowered(hidden, coefficient, down_ref, first, count):
    columns = down_ref[0, :, first : first + count]
    return jnp.dot(hidden, columns, preferred_element_type=jnp.float32) * coefficient


def early_kernel(*refs):
    *refs, keep_ref, give_ref, side_keep_ref, side_give_ref = refs
    *others, side_ref, side_beside_ref, gate_ref, up_ref, down_ref = refs
    lows, highs = zip(*[halves(ref) for ref in others])
    side_low, side_high = ordered(wide(side_ref), wide(side_beside_ref))
    hidden, coefficient = hidden_rows(
        [*lows, side_low], [*highs, side_high], gate_ref, up_ref
    )
    rows, width = keep_ref.shape
    end = rows + give_ref.shape[0]
    half = width // 2
    step = half // 2
    for start in range(0, half, step):
        low = lowered(hidden, coefficient, down_ref, start, step)
        high = lowered(hidden, coefficient, down_ref, half + start, step)
        for value, first in ((low, start), (high, half + start)):
            keep_ref[:, first : first + step] = value[:rows]
            give_ref[:, first : first + step] = value[rows:end].astype(jnp.bfloat16)
        keep, give = ordered(low[end:], high[end:])
        side_keep_ref[:, start : start + step] = keep
        side_give_ref[:, start : start + step] = give.astype(jnp.bfloat16)


def low_kernel(*refs):
    *others, gate_ref, up_ref, down_ref, give_ref, hidden_ref, coefficient_ref = refs
    lows, highs = zip(*[halves(ref) for ref in others])
    hidden, coefficient = hidden_rows(lows, highs, gate_ref, up_ref)
    hidden_ref[...] = hidden
    coefficient_ref[...] = jnp.broadcast_to(coefficient, coefficient_ref.shape)
    rows, half = give_ref.shape
    step = half // 2
    for start in range(0, half, step):
        low = lowered(hidden[:rows], coefficient[:rows], down_ref, start, step)
        give_ref[:, start : start + step] = low.astype(jnp.bfloat16)


def high_kernel(hidden_ref, coefficient_ref, down_ref, give_ref):
    rows, half = give_ref.shape
    hidden, coefficient = hidden_ref[:rows, :], coefficient_ref[:rows, :1]
    step = half // 2
    for start in range(0, half, step):
        high = lowered(hidden, coefficient, down_ref, half + start, step)
        give_ref[:, start : start + step] = high.astype(jnp.bfloat16)


def kept_kernel(hidden_ref, coefficient_ref, down_ref, keep_ref):
    rows, width = keep_ref.shape
    hidden, coefficient = hidden_ref[rows:, :], coefficient_ref[rows:, :1]
    step = width // 4
    for start in range(0, width, step):
        keep_ref[:, start : start + step] = lowered(hidden, coefficient, down_ref, start, step)


def early_fold_kernel(*refs):
    keep_ref, other_ref, side_keep_ref, side_other_ref, *outs, side_out_ref = refs
    count = side_out_ref.shape[0]
    side_out_ref[...] = (side_keep_ref[...] + wide(side_other_ref)).astype(jnp.bfloat16)
    for j, out_ref in enumerate(outs):
        total = keep_ref[(j + 1) * count : (j + 2) * count, :]
        total += other_ref[j * count : (j + 1) * count, :].astype(jnp.float32)
        out_ref[...] = total.astype(jnp.bfloat16)


def fold_kernel(*refs):
    keep_ref, low_ref, high_ref, *outs = refs
    half = low_ref.shape[1]
    count = outs[0].shape[0]
    for j, out_ref in enumerate(outs):
        rows = slice(j * count, (j + 1) * count)
        low = keep_ref[rows, :half] + low_ref[rows, :].astype(jnp.float32)
        high = keep_ref[rows, half:] + high_ref[rows, :].astype(jnp.float32)
        out_ref[:, :half] = low.astype(jnp.bfloat16)
        out_ref[:, half:] = high.astype(jnp.bfloat16)


def sum_kernel(*refs):
    keep_ref, side_ref, *parts, mine_ref, give_ref = refs
    rows, half = side_ref.shape
    tokens = rows // 4
    total = keep_ref[:rows, :]
    for ref in parts:
        total += wide(ref)
    side = wide(side_ref)
    zero = jnp.zeros_like(side)
    total += jnp.concatenate(ordered(side, zero), axis=1)
    near = ordered(total[:tokens], total[tokens : 2 * tokens])
    far = ordered(total[2 * tokens : 3 * tokens], total[3 * tokens :])

    def folded(which):
        columns = (slice(0, half), slice(half, 2 * half))
        return jnp.concatenate([b[which][:, c] for c in columns for b in (near, far)], axis=0)

    mine_ref[...] = folded(0)
    give_ref[...] = folded(1).astype(jnp.bfloat16)


def split_kernel(mine_ref, other_ref, near_ref, far_ref):
    total = mine_ref[...] + wide(other_ref)
    tokens = total.shape[0] // 4
    piece = near_ref.shape[1]

    def folded(which):
        pieces = []
        for side in range(2):
            start = (2 * side + which) * tokens
            rows = total[start : start + tokens]
            pieces += [rows[:, :piece], rows[:, piece:]]
        return jnp.concatenate(pieces, axis=0)

    near_ref[...] = folded(0)
    far_ref[...] = folded(1).astype(jnp.bfloat16)


def finish_kernel(near_ref, other_ref, out_ref):
    tokens, width = out_ref.shape
    piece = width // PARTS
    total = near_ref[...] + wide(other_ref)
    for p in range(PARTS):
        rows = total[p * tokens : (p + 1) * tokens]
        out_ref[:, p * piece : (p + 1) * piece] = rows.astype(jnp.bfloat16)


def body(hidden_states, norm_gain, gate_scores, routes, draft_counts, w_gate, w_up, w_down):
    tokens, width = hidden_states.shape
    devices = lax.axis_size("ep")
    far = devices // 2
    shared = far - 2
    steps = [(hop, shared ^ hop) for hop in range(2, far // 2, 2)]
    half, piece = width // 2, width // PARTS
    extra = lane_round(far)
    shape = jax.ShapeDtypeStruct
    bf16, f32 = jnp.bfloat16, jnp.float32
    inner = w_gate.shape[2]

    small = [
        pltpu.with_memory_space_constraint(a, pltpu.HBM)
        for a in (draft_counts, hidden_states, norm_gain, gate_scores, routes)
    ]
    packed = call(
        pack_kernel,
        [shape((PARTS * tokens, piece + extra), bf16)],
        4 * MIB,
        *small,
        specs=[HBM] * 5,
        scratch=[pltpu.SMEM(draft_counts.shape, jnp.int32)]
        + [pltpu.VMEM(a.shape, a.dtype) for a in small[1:]]
        + [pltpu.SemaphoreType.DMA((5,))],
    )
    moved = swapped(packed, far)
    beside = swapped(packed, 1)
    weights = [pltpu.with_memory_space_constraint(w, pltpu.HBM) for w in (w_gate, w_up, w_down)]
    *loaded, token = call(
        load_kernel,
        [pltpu.VMEM(w.shape, w.dtype) for w in weights] + [shape((8, 128), f32)],
        MIB,
        *weights,
        specs=[HBM] * 3,
        scratch=[pltpu.SemaphoreType.DMA((3,))],
    )
    loaded = [pltpu.with_memory_space_constraint(w, pltpu.VMEM) for w in loaded]
    rows = 4 * tokens
    block, side = call(
        combine_kernel,
        [shape((rows, width + 2 * extra), bf16), shape((rows, half + extra), bf16)],
        4 * MIB,
        packed,
        beside,
        moved,
        swapped(moved, 1),
        token,
        specs=[VMEM] * 4 + [ANY],
    )
    side = swapped(side, shared)
    parts = [swapped(block, *step) for step in steps]
    side_beside = swapped(side, 1)
    beside = [swapped(part, 1) for part in parts]
    early = early_count(devices)
    late = len(steps) - early
    work = 2 * rows * width * inner
    keep, give, side_keep, side_give = call(
        early_kernel,
        [
            shape(((1 + early) * rows, width), f32),
            shape((early * rows, width), bf16),
            shape((rows, half), f32),
            shape((rows, half), bf16),
        ],
        16 * MIB,
        block,
        *parts[:early],
        *beside[:early],
        side,
        side_beside,
        *loaded,
        flops=3 * (2 + 2 * early) * work,
    )
    *first_parts, side = call(
        early_fold_kernel,
        [shape((rows, width), bf16)] * early + [shape((rows, half), bf16)],
        8 * MIB,
        keep,
        swapped(give, 1),
        side_keep,
        swapped(side_give, 1),
    )
    low, hidden, coefficient = call(
        low_kernel,
        [
            shape((late * rows, half), bf16),
            shape((2 * late * rows, inner), bf16),
            shape((2 * late * rows, 128), f32),
        ],
        16 * MIB,
        *beside[early:],
        *parts[early:],
        *loaded,
        flops=9 * late * work // 2,
    )
    low = swapped(low, 1)
    high = call(
        high_kernel,
        [shape((late * rows, half), bf16)],
        8 * MIB,
        hidden,
        coefficient,
        loaded[2],
        flops=late * work // 2,
    )
    high = swapped(high, 1)
    late_keep = call(
        kept_kernel,
        [shape((late * rows, width), f32)],
        8 * MIB,
        hidden,
        coefficient,
        loaded[2],
        flops=late * work,
    )
    parts = call(fold_kernel, [shape((rows, width), bf16)] * late, 8 * MIB, late_keep, low, high)
    parts = [*first_parts, *parts]
    side = swapped(side, shared)
    parts = [swapped(part, *step) for part, step in zip(parts, steps)]
    mine, give = call(
        sum_kernel,
        [shape((rows, half), f32), shape((rows, half), bf16)],
        8 * MIB,
        keep,
        side,
        *parts,
    )
    near, give = call(
        split_kernel,
        [shape((PARTS * tokens, piece), f32), shape((PARTS * tokens, piece), bf16)],
        4 * MIB,
        mine,
        swapped(give, 1),
    )
    return call(finish_kernel, [shape((tokens, width), bf16)], 4 * MIB, near, swapped(give, far))


def early_count(devices):
    return max(1, (devices // 8 - 1) // 3)


def solution(mesh):
    return jax.shard_map(
        body,
        mesh=mesh,
        in_specs=(
            P(("grp", "ep"), None),
            P(),
            P(("grp", "ep"), None),
            P(("grp", "ep"), None),
            P(("grp", "ep")),
            P("ep", None, None),
            P("ep", None, None),
            P("ep", None, None),
        ),
        out_specs=P(("grp", "ep"), None),
        check_vma=False,
    )
```

```python
import math

import jax
import jax.numpy as jnp
from jax import lax
from jax.experimental import pallas as pl
from jax.experimental.pallas import tpu as pltpu
from jax.sharding import PartitionSpec as P


VMEM = pl.BlockSpec(memory_space=pltpu.VMEM)
ANY = pl.BlockSpec(memory_space=pl.ANY)
HBM = pl.BlockSpec(memory_space=pltpu.HBM)
PARTS = 4
MIB = 1024 * 1024


def swapped(array, *distances):
    size = lax.axis_size("ep")
    pairs = [(i, i ^ distances[i % len(distances)]) for i in range(size)]
    return lax.ppermute(array, "ep", pairs)


def core():
    return lax.rem(lax.axis_index("ep"), 2)


def ordered(own, other):
    first = core() == 0
    return jnp.where(first, own, other), jnp.where(first, other, own)


def wide(ref):
    return ref[...].astype(jnp.float32)


def lane_round(count):
    return -(-count // 128) * 128


def call(kernel, outs, limit, *args, specs=None, flops=0, scratch=()):
    moved = sum(math.prod(a.shape) * a.dtype.itemsize for a in (*args, *outs))
    single = len(outs) == 1
    return pl.pallas_call(
        kernel,
        out_shape=outs[0] if single else tuple(outs),
        in_specs=specs or [VMEM] * len(args),
        out_specs=VMEM if single else tuple([VMEM] * len(outs)),
        scratch_shapes=list(scratch),
        compiler_params=pltpu.CompilerParams(vmem_limit_bytes=limit),
        cost_estimate=pl.CostEstimate(flops=flops, bytes_accessed=moved, transcendentals=0),
    )(*args)


def pack_kernel(
    draft_hbm, states_hbm, gain_hbm, scores_hbm, routes_hbm, out_ref,
    draft_ref, states_ref, gain_ref, scores_ref, routes_ref, sems,
):
    sources = (draft_hbm, states_hbm, gain_hbm, scores_hbm, routes_hbm)
    targets = (draft_ref, states_ref, gain_ref, scores_ref, routes_ref)
    copies = [
        pltpu.make_async_copy(source, target, sems.at[i])
        for i, (source, target) in enumerate(zip(sources, targets))
    ]
    for copy in copies:
        copy.start()
    for copy in copies:
        copy.wait()
    tokens, width = states_ref.shape
    piece = width // PARTS
    extra = out_ref.shape[1] - piece
    requests = draft_ref.shape[0]
    slots = tokens // requests
    states = wide(states_ref)
    mean_square = jnp.mean(states * states, axis=-1, keepdims=True)
    normed = (states * lax.rsqrt(mean_square + 1e-06) * gain_ref[...].reshape(1, width)).astype(jnp.bfloat16)
    scores = scores_ref[...]
    weights = 2.5 * scores / jnp.sum(scores, axis=-1, keepdims=True)
    row = lax.broadcasted_iota(jnp.int32, (tokens, 1), 0)
    live = jnp.zeros((tokens, 1), jnp.bool_)
    for request in range(requests):
        inside = (row >= request * slots) & (row <= request * slots + draft_ref[request])
        live = live | (inside & (row < (request + 1) * slots))
    weights = jnp.where(live, weights, 0.0)
    lane = lax.broadcasted_iota(jnp.int32, (tokens, extra), 1)
    coefficient = jnp.zeros((tokens, extra), jnp.float32)
    for k in range(routes_ref.shape[1]):
        coefficient += jnp.where(routes_ref[:, k : k + 1] == lane, weights[:, k : k + 1], 0.0)
    coarse = coefficient.astype(jnp.bfloat16)
    fine = (coefficient - coarse.astype(jnp.float32)).astype(jnp.bfloat16)
    zero = jnp.zeros((tokens, extra), jnp.float32)
    coarse, fine = coarse.astype(jnp.float32), fine.astype(jnp.float32)
    sides = [coarse, fine] + [zero] * (PARTS - 2)
    normed = normed.astype(jnp.float32)
    normed = jnp.concatenate([normed[:, p * piece : (p + 1) * piece] for p in range(PARTS)], axis=0)
    rows = jnp.concatenate([normed, jnp.concatenate(sides, axis=0)], axis=1).astype(jnp.bfloat16)
    out_ref[...] = rows


def load_kernel(*refs):
    count = (len(refs) - 2) // 2
    token_ref, sems = refs[-2:]
    token_ref[...] = jnp.zeros_like(token_ref)
    copies = [
        pltpu.make_async_copy(refs[i], refs[count + i], sems.at[i]) for i in range(count)
    ]
    for copy in copies:
        copy.start()
    for copy in copies:
        copy.wait()


def combine_kernel(own_ref, beside_ref, far_ref, far_beside_ref, after_ref, out_ref, side_ref):
    tokens = own_ref.shape[0] // PARTS
    piece = own_ref.shape[1] - (PARTS * own_ref.shape[1] - out_ref.shape[1]) // 2

    def unfolded(rows):
        parts = [rows[p * tokens : (p + 1) * tokens] for p in range(PARTS)]
        columns = []
        for side in range(2):
            columns += [p[:, :piece] for p in parts[2 * side : 2 * side + 2]]
            columns.append(parts[side][:, piece:])
        return jnp.concatenate(columns, axis=1)

    blocks = ordered(wide(own_ref), wide(beside_ref)) + ordered(wide(far_ref), wide(far_beside_ref))
    rows = jnp.concatenate([unfolded(b) for b in blocks], axis=0)
    out_ref[...] = rows.astype(jnp.bfloat16)
    middle = rows.shape[1] // 2
    side_ref[...] = ordered(rows[:, :middle], rows[:, middle:])[0].astype(jnp.bfloat16)


def hidden_rows(lows, highs, gate_ref, up_ref):
    half = gate_ref.shape[1] // 2
    low, high = jnp.concatenate(lows, axis=0), jnp.concatenate(highs, axis=0)
    mixed = low[:, half:] + high[:, half:]
    lane = lax.broadcasted_iota(jnp.int32, mixed.shape, 1)
    expert = lax.axis_index("ep") // 2
    coefficient = jnp.sum(jnp.where(lane == expert, mixed, 0.0), axis=1, keepdims=True)
    low = low[:, :half].astype(jnp.bfloat16)
    high = high[:, :half].astype(jnp.bfloat16)

    def projected(ref):
        first = jnp.dot(low, ref[0, :half], preferred_element_type=jnp.float32)
        return first + jnp.dot(high, ref[0, half:], preferred_element_type=jnp.float32)

    gate = projected(gate_ref)
    up = projected(up_ref)
    return (gate / (1.0 + jnp.exp(-gate)) * up).astype(jnp.bfloat16), coefficient


def halves(ref):
    middle = ref.shape[1] // 2
    return ref[:, :middle].astype(jnp.float32), ref[:, middle:].astype(jnp.float32)


def lowered(hidden, coefficient, down_ref, first, count):
    columns = down_ref[0, :, first : first + count]
    return jnp.dot(hidden, columns, preferred_element_type=jnp.float32) * coefficient


def early_kernel(*refs):
    *refs, keep_ref, give_ref, side_keep_ref, side_give_ref = refs
    *others, side_ref, side_beside_ref, gate_ref, up_ref, down_ref = refs
    lows, highs = zip(*[halves(ref) for ref in others])
    side_low, side_high = ordered(wide(side_ref), wide(side_beside_ref))
    hidden, coefficient = hidden_rows(
        [*lows, side_low], [*highs, side_high], gate_ref, up_ref
    )
    rows, width = keep_ref.shape
    end = rows + give_ref.shape[0]
    half = width // 2
    step = half // 2
    for start in range(0, half, step):
        low = lowered(hidden, coefficient, down_ref, start, step)
        high = lowered(hidden, coefficient, down_ref, half + start, step)
        for value, first in ((low, start), (high, half + start)):
            keep_ref[:, first : first + step] = value[:rows]
            give_ref[:, first : first + step] = value[rows:end].astype(jnp.bfloat16)
        keep, give = ordered(low[end:], high[end:])
        side_keep_ref[:, start : start + step] = keep
        side_give_ref[:, start : start + step] = give.astype(jnp.bfloat16)


def late_kernel(*refs):
    *others, gate_ref, up_ref, down_ref, keep_ref, give_ref = refs
    lows, highs = zip(*[halves(ref) for ref in others])
    hidden, coefficient = hidden_rows(lows, highs, gate_ref, up_ref)
    rows, width = keep_ref.shape
    step = width // 4
    for start in range(0, width, step):
        partial = lowered(hidden, coefficient, down_ref, start, step)
        keep_ref[:, start : start + step] = partial[:rows]
        give_ref[:, start : start + step] = partial[rows:].astype(jnp.bfloat16)


def early_fold_kernel(*refs):
    keep_ref, other_ref, side_keep_ref, side_other_ref, *outs, side_out_ref = refs
    count = side_out_ref.shape[0]
    side_out_ref[...] = (side_keep_ref[...] + wide(side_other_ref)).astype(jnp.bfloat16)
    for j, out_ref in enumerate(outs):
        total = keep_ref[(j + 1) * count : (j + 2) * count, :]
        total += other_ref[j * count : (j + 1) * count, :].astype(jnp.float32)
        out_ref[...] = total.astype(jnp.bfloat16)


def fold_kernel(keep_ref, other_ref, *outs):
    count = outs[0].shape[0]
    for j, out_ref in enumerate(outs):
        rows = slice(j * count, (j + 1) * count)
        total = keep_ref[rows, :] + other_ref[rows, :].astype(jnp.float32)
        out_ref[...] = total.astype(jnp.bfloat16)


def sum_kernel(*refs):
    keep_ref, side_ref, *parts, mine_ref, give_ref = refs
    rows, half = side_ref.shape
    tokens = rows // 4
    total = keep_ref[:rows, :]
    for ref in parts:
        total += wide(ref)
    side = wide(side_ref)
    zero = jnp.zeros_like(side)
    total += jnp.concatenate(ordered(side, zero), axis=1)
    near = ordered(total[:tokens], total[tokens : 2 * tokens])
    far = ordered(total[2 * tokens : 3 * tokens], total[3 * tokens :])

    def folded(which):
        columns = (slice(0, half), slice(half, 2 * half))
        return jnp.concatenate([b[which][:, c] for c in columns for b in (near, far)], axis=0)

    mine_ref[...] = folded(0)
    give_ref[...] = folded(1).astype(jnp.bfloat16)


def split_kernel(mine_ref, other_ref, near_ref, far_ref):
    total = mine_ref[...] + wide(other_ref)
    tokens = total.shape[0] // 4
    piece = near_ref.shape[1]

    def folded(which):
        pieces = []
        for side in range(2):
            start = (2 * side + which) * tokens
            rows = total[start : start + tokens]
            pieces += [rows[:, :piece], rows[:, piece:]]
        return jnp.concatenate(pieces, axis=0)

    near_ref[...] = folded(0)
    far_ref[...] = folded(1).astype(jnp.bfloat16)


def finish_kernel(near_ref, other_ref, out_ref):
    tokens, width = out_ref.shape
    piece = width // PARTS
    total = near_ref[...] + wide(other_ref)
    for p in range(PARTS):
        rows = total[p * tokens : (p + 1) * tokens]
        out_ref[:, p * piece : (p + 1) * piece] = rows.astype(jnp.bfloat16)


def body(hidden_states, norm_gain, gate_scores, routes, draft_counts, w_gate, w_up, w_down):
    tokens, width = hidden_states.shape
    devices = lax.axis_size("ep")
    far = devices // 2
    shared = far - 2
    steps = [(hop, shared ^ hop) for hop in range(2, far // 2, 2)]
    half, piece = width // 2, width // PARTS
    extra = lane_round(far)
    shape = jax.ShapeDtypeStruct
    bf16, f32 = jnp.bfloat16, jnp.float32
    inner = w_gate.shape[2]

    small = [
        pltpu.with_memory_space_constraint(a, pltpu.HBM)
        for a in (draft_counts, hidden_states, norm_gain, gate_scores, routes)
    ]
    packed = call(
        pack_kernel,
        [shape((PARTS * tokens, piece + extra), bf16)],
        4 * MIB,
        *small,
        specs=[HBM] * 5,
        scratch=[pltpu.SMEM(draft_counts.shape, jnp.int32)]
        + [pltpu.VMEM(a.shape, a.dtype) for a in small[1:]]
        + [pltpu.SemaphoreType.DMA((5,))],
    )
    moved = swapped(packed, far)
    beside = swapped(packed, 1)
    weights = [pltpu.with_memory_space_constraint(w, pltpu.HBM) for w in (w_gate, w_up, w_down)]
    *loaded, token = call(
        load_kernel,
        [pltpu.VMEM(w.shape, w.dtype) for w in weights] + [shape((8, 128), f32)],
        MIB,
        *weights,
        specs=[HBM] * 3,
        scratch=[pltpu.SemaphoreType.DMA((3,))],
    )
    loaded = [pltpu.with_memory_space_constraint(w, pltpu.VMEM) for w in loaded]
    rows = 4 * tokens
    block, side = call(
        combine_kernel,
        [shape((rows, width + 2 * extra), bf16), shape((rows, half + extra), bf16)],
        4 * MIB,
        packed,
        beside,
        moved,
        swapped(moved, 1),
        token,
        specs=[VMEM] * 4 + [ANY],
    )
    side = swapped(side, shared)
    parts = [swapped(block, *step) for step in steps]
    side_beside = swapped(side, 1)
    beside = [swapped(part, 1) for part in parts]
    early = early_count(devices)
    late = len(steps) - early
    work = 2 * rows * width * inner
    keep, give, side_keep, side_give = call(
        early_kernel,
        [
            shape(((1 + early) * rows, width), f32),
            shape((early * rows, width), bf16),
            shape((rows, half), f32),
            shape((rows, half), bf16),
        ],
        16 * MIB,
        block,
        *parts[:early],
        *beside[:early],
        side,
        side_beside,
        *loaded,
        flops=3 * (2 + 2 * early) * work,
    )
    *first_parts, side = call(
        early_fold_kernel,
        [shape((rows, width), bf16)] * early + [shape((rows, half), bf16)],
        8 * MIB,
        keep,
        swapped(give, 1),
        side_keep,
        swapped(side_give, 1),
    )
    late_keep, late_give = call(
        late_kernel,
        [shape((late * rows, width), f32), shape((late * rows, width), bf16)],
        16 * MIB,
        *parts[early:],
        *beside[early:],
        *loaded,
        flops=6 * late * work,
    )
    parts = call(
        fold_kernel, [shape((rows, width), bf16)] * late, 8 * MIB, late_keep, swapped(late_give, 1)
    )
    parts = [*first_parts, *parts]
    side = swapped(side, shared)
    parts = [swapped(part, *step) for part, step in zip(parts, steps)]
    mine, give = call(
        sum_kernel,
        [shape((rows, half), f32), shape((rows, half), bf16)],
        8 * MIB,
        keep,
        side,
        *parts,
    )
    near, give = call(
        split_kernel,
        [shape((PARTS * tokens, piece), f32), shape((PARTS * tokens, piece), bf16)],
        4 * MIB,
        mine,
        swapped(give, 1),
    )
    return call(finish_kernel, [shape((tokens, width), bf16)], 4 * MIB, near, swapped(give, far))


def early_count(devices):
    return max(1, (devices // 8 - 1) // 3)


def solution(mesh):
    return jax.shard_map(
        body,
        mesh=mesh,
        in_specs=(
            P(("grp", "ep"), None),
            P(),
            P(("grp", "ep"), None),
            P(("grp", "ep"), None),
            P(("grp", "ep")),
            P("ep", None, None),
            P("ep", None, None),
            P("ep", None, None),
        ),
        out_specs=P(("grp", "ep"), None),
        check_vma=False,
    )
```

```python
import functools
import math

import jax
import jax.numpy as jnp
from jax import lax
from jax.experimental import pallas as pl
from jax.experimental.pallas import tpu as pltpu
from jax.sharding import PartitionSpec as P


VMEM = pl.BlockSpec(memory_space=pltpu.VMEM)
ANY = pl.BlockSpec(memory_space=pl.ANY)
HBM = pl.BlockSpec(memory_space=pltpu.HBM)
PARTS = 4
MIB = 1024 * 1024


def swapped(array, *distances):
    size = lax.axis_size("ep")
    pairs = [(i, i ^ distances[i % len(distances)]) for i in range(size)]
    return lax.ppermute(array, "ep", pairs)


def core():
    return lax.rem(lax.axis_index("ep"), 2)


def ordered(own, other):
    first = core() == 0
    return jnp.where(first, own, other), jnp.where(first, other, own)


def wide(ref):
    return ref[...].astype(jnp.float32)


def lane_round(count):
    return -(-count // 128) * 128


def call(kernel, outs, limit, *args, specs=None, flops=0, scratch=()):
    moved = sum(math.prod(a.shape) * a.dtype.itemsize for a in (*args, *outs))
    single = len(outs) == 1
    return pl.pallas_call(
        kernel,
        out_shape=outs[0] if single else tuple(outs),
        in_specs=specs or [VMEM] * len(args),
        out_specs=VMEM if single else tuple([VMEM] * len(outs)),
        scratch_shapes=list(scratch),
        compiler_params=pltpu.CompilerParams(vmem_limit_bytes=limit),
        cost_estimate=pl.CostEstimate(flops=flops, bytes_accessed=moved, transcendentals=0),
    )(*args)


def pack_kernel(
    draft_hbm, states_hbm, gain_hbm, scores_hbm, routes_hbm, out_ref,
    draft_ref, states_ref, gain_ref, scores_ref, routes_ref, sems,
):
    sources = (draft_hbm, states_hbm, gain_hbm, scores_hbm, routes_hbm)
    targets = (draft_ref, states_ref, gain_ref, scores_ref, routes_ref)
    copies = [
        pltpu.make_async_copy(source, target, sems.at[i])
        for i, (source, target) in enumerate(zip(sources, targets))
    ]
    for copy in copies:
        copy.start()
    for copy in copies:
        copy.wait()
    tokens, width = states_ref.shape
    piece = width // PARTS
    extra = out_ref.shape[1] - piece
    requests = draft_ref.shape[0]
    slots = tokens // requests
    states = wide(states_ref)
    mean_square = jnp.mean(states * states, axis=-1, keepdims=True)
    normed = (states * lax.rsqrt(mean_square + 1e-06) * gain_ref[...].reshape(1, width)).astype(jnp.bfloat16)
    scores = scores_ref[...]
    weights = 2.5 * scores / jnp.sum(scores, axis=-1, keepdims=True)
    row = lax.broadcasted_iota(jnp.int32, (tokens, 1), 0)
    live = jnp.zeros((tokens, 1), jnp.bool_)
    for request in range(requests):
        inside = (row >= request * slots) & (row <= request * slots + draft_ref[request])
        live = live | (inside & (row < (request + 1) * slots))
    weights = jnp.where(live, weights, 0.0)
    lane = lax.broadcasted_iota(jnp.int32, (tokens, extra), 1)
    coefficient = jnp.zeros((tokens, extra), jnp.float32)
    for k in range(routes_ref.shape[1]):
        coefficient += jnp.where(routes_ref[:, k : k + 1] == lane, weights[:, k : k + 1], 0.0)
    coarse = coefficient.astype(jnp.bfloat16)
    fine = (coefficient - coarse.astype(jnp.float32)).astype(jnp.bfloat16)
    zero = jnp.zeros((tokens, extra), jnp.float32)
    coarse, fine = coarse.astype(jnp.float32), fine.astype(jnp.float32)
    sides = [coarse, fine] + [zero] * (PARTS - 2)
    normed = normed.astype(jnp.float32)
    normed = jnp.concatenate([normed[:, p * piece : (p + 1) * piece] for p in range(PARTS)], axis=0)
    rows = jnp.concatenate([normed, jnp.concatenate(sides, axis=0)], axis=1).astype(jnp.bfloat16)
    out_ref[...] = rows


def load_kernel(*refs):
    count = (len(refs) - 2) // 2
    token_ref, sems = refs[-2:]
    token_ref[...] = jnp.zeros_like(token_ref)
    copies = [
        pltpu.make_async_copy(refs[i], refs[count + i], sems.at[i]) for i in range(count)
    ]
    for copy in copies:
        copy.start()
    for copy in copies:
        copy.wait()


def combine_kernel(own_ref, beside_ref, far_ref, far_beside_ref, after_ref, out_ref, side_ref):
    tokens = own_ref.shape[0] // PARTS
    piece = own_ref.shape[1] - (PARTS * own_ref.shape[1] - out_ref.shape[1]) // 2

    def unfolded(rows):
        parts = [rows[p * tokens : (p + 1) * tokens] for p in range(PARTS)]
        columns = []
        for side in range(2):
            columns += [p[:, :piece] for p in parts[2 * side : 2 * side + 2]]
            columns.append(parts[side][:, piece:])
        return jnp.concatenate(columns, axis=1)

    blocks = ordered(wide(own_ref), wide(beside_ref)) + ordered(wide(far_ref), wide(far_beside_ref))
    rows = jnp.concatenate([unfolded(b) for b in blocks], axis=0)
    out_ref[...] = rows.astype(jnp.bfloat16)
    middle = rows.shape[1] // 2
    side_ref[...] = ordered(rows[:, :middle], rows[:, middle:])[0].astype(jnp.bfloat16)


def hidden_rows(lows, highs, gate_ref, up_ref):
    half = gate_ref.shape[1] // 2
    low, high = jnp.concatenate(lows, axis=0), jnp.concatenate(highs, axis=0)
    mixed = low[:, half:] + high[:, half:]
    lane = lax.broadcasted_iota(jnp.int32, mixed.shape, 1)
    expert = lax.axis_index("ep") // 2
    coefficient = jnp.sum(jnp.where(lane == expert, mixed, 0.0), axis=1, keepdims=True)
    low = low[:, :half].astype(jnp.bfloat16)
    high = high[:, :half].astype(jnp.bfloat16)

    def projected(ref):
        first = jnp.dot(low, ref[0, :half], preferred_element_type=jnp.float32)
        return first + jnp.dot(high, ref[0, half:], preferred_element_type=jnp.float32)

    gate = projected(gate_ref)
    up = projected(up_ref)
    return (gate / (1.0 + jnp.exp(-gate)) * up).astype(jnp.bfloat16), coefficient


def halves(ref):
    middle = ref.shape[1] // 2
    return ref[:, :middle].astype(jnp.float32), ref[:, middle:].astype(jnp.float32)


def lowered(hidden, coefficient, down_ref, first, count):
    columns = down_ref[0, :, first : first + count]
    return jnp.dot(hidden, columns, preferred_element_type=jnp.float32) * coefficient


def early_kernel(*refs):
    *refs, keep_ref, give_ref, side_keep_ref, side_give_ref = refs
    *others, side_ref, side_beside_ref, gate_ref, up_ref, down_ref = refs
    lows, highs = zip(*[halves(ref) for ref in others])
    side_low, side_high = ordered(wide(side_ref), wide(side_beside_ref))
    hidden, coefficient = hidden_rows(
        [*lows, side_low], [*highs, side_high], gate_ref, up_ref
    )
    rows, width = keep_ref.shape
    end = rows + give_ref.shape[0]
    half = width // 2
    step = half // 2
    for start in range(0, half, step):
        low = lowered(hidden, coefficient, down_ref, start, step)
        high = lowered(hidden, coefficient, down_ref, half + start, step)
        for value, first in ((low, start), (high, half + start)):
            keep_ref[:, first : first + step] = value[:rows]
            give_ref[:, first : first + step] = value[rows:end].astype(jnp.bfloat16)
        keep, give = ordered(low[end:], high[end:])
        side_keep_ref[:, start : start + step] = keep
        side_give_ref[:, start : start + step] = give.astype(jnp.bfloat16)


def late_kernel(*refs):
    *others, gate_ref, up_ref, down_ref, keep_ref, give_ref = refs
    lows, highs = zip(*[halves(ref) for ref in others])
    hidden, coefficient = hidden_rows(lows, highs, gate_ref, up_ref)
    rows, width = keep_ref.shape
    step = width // 4
    for start in range(0, width, step):
        partial = lowered(hidden, coefficient, down_ref, start, step)
        keep_ref[:, start : start + step] = partial[:rows]
        give_ref[:, start : start + step] = partial[rows:].astype(jnp.bfloat16)


def early_fold_kernel(*refs):
    keep_ref, other_ref, side_keep_ref, side_other_ref, *outs, side_out_ref = refs
    count = side_out_ref.shape[0]
    side_out_ref[...] = (side_keep_ref[...] + wide(side_other_ref)).astype(jnp.bfloat16)
    for j, out_ref in enumerate(outs):
        total = keep_ref[(j + 1) * count : (j + 2) * count, :]
        total += other_ref[j * count : (j + 1) * count, :].astype(jnp.float32)
        out_ref[...] = total.astype(jnp.bfloat16)


def fold_kernel(keep_ref, other_ref, *outs):
    rows, half = outs[0].shape
    count = rows // 2
    total = keep_ref[...] + wide(other_ref)
    for j, out_ref in enumerate(outs):
        part = total[j * count : (j + 1) * count]
        both = jnp.concatenate([part[:, :half], part[:, half:]], axis=0)
        out_ref[...] = both.astype(jnp.bfloat16)


def sum_kernel(place, early, *refs):
    keep_ref, side_ref, *parts, mine_ref, give_ref = refs
    count, half = side_ref.shape[0] // 2, side_ref.shape[1]
    tokens = count // 2
    piece = half // 2
    rows = slice(place * count, (place + 1) * count)
    total = keep_ref[rows, :]
    for ref in parts[:early]:
        total += wide(ref)[rows]
    total = jnp.concatenate([total[:, :half], total[:, half:]], axis=0)
    side = wide(side_ref)[rows]
    total += jnp.concatenate(ordered(side, jnp.zeros_like(side)), axis=0)
    for ref in parts[early:]:
        total += wide(ref)
    quarters = [total[q * tokens : (q + 1) * tokens] for q in range(4)]
    pairs = [ordered(quarters[0], quarters[1]), ordered(quarters[2], quarters[3])]

    def folded(which):
        pieces = [pair[which][:, c : c + piece] for pair in pairs for c in (0, piece)]
        return jnp.concatenate(pieces, axis=0)

    mine_ref[...] = folded(0)
    give_ref[...] = folded(1).astype(jnp.bfloat16)


def add_kernel(mine_ref, other_ref, out_ref):
    out_ref[...] = (mine_ref[...] + wide(other_ref)).astype(out_ref.dtype)


def finish_kernel(near_ref, beside_ref, other_ref, out_ref):
    tokens, width = out_ref.shape
    piece = width // PARTS
    total = near_ref[...] + wide(beside_ref) + wide(other_ref)
    for p in range(PARTS):
        rows = total[p * tokens : (p + 1) * tokens]
        out_ref[:, p * piece : (p + 1) * piece] = rows.astype(jnp.bfloat16)


def body(hidden_states, norm_gain, gate_scores, routes, draft_counts, w_gate, w_up, w_down):
    tokens, width = hidden_states.shape
    devices = lax.axis_size("ep")
    far = devices // 2
    shared = far - 2
    steps = [(hop, shared ^ hop) for hop in range(2, far // 2, 2)]
    half, piece = width // 2, width // PARTS
    extra = lane_round(far)
    shape = jax.ShapeDtypeStruct
    bf16, f32 = jnp.bfloat16, jnp.float32
    inner = w_gate.shape[2]

    small = [
        pltpu.with_memory_space_constraint(a, pltpu.HBM)
        for a in (draft_counts, hidden_states, norm_gain, gate_scores, routes)
    ]
    packed = call(
        pack_kernel,
        [shape((PARTS * tokens, piece + extra), bf16)],
        4 * MIB,
        *small,
        specs=[HBM] * 5,
        scratch=[pltpu.SMEM(draft_counts.shape, jnp.int32)]
        + [pltpu.VMEM(a.shape, a.dtype) for a in small[1:]]
        + [pltpu.SemaphoreType.DMA((5,))],
    )
    moved = swapped(packed, far)
    beside = swapped(packed, 1)
    weights = [pltpu.with_memory_space_constraint(w, pltpu.HBM) for w in (w_gate, w_up, w_down)]
    *loaded, token = call(
        load_kernel,
        [pltpu.VMEM(w.shape, w.dtype) for w in weights] + [shape((8, 128), f32)],
        MIB,
        *weights,
        specs=[HBM] * 3,
        scratch=[pltpu.SemaphoreType.DMA((3,))],
    )
    loaded = [pltpu.with_memory_space_constraint(w, pltpu.VMEM) for w in loaded]
    rows = 4 * tokens
    block, side = call(
        combine_kernel,
        [shape((rows, width + 2 * extra), bf16), shape((rows, half + extra), bf16)],
        4 * MIB,
        packed,
        beside,
        moved,
        swapped(moved, 1),
        token,
        specs=[VMEM] * 4 + [ANY],
    )
    side = swapped(side, shared)
    parts = [swapped(block, *step) for step in steps]
    side_beside = swapped(side, 1)
    beside = [swapped(part, 1) for part in parts]
    early = early_count(devices)
    late = len(steps) - early
    work = 2 * rows * width * inner
    keep, give, side_keep, side_give = call(
        early_kernel,
        [
            shape(((1 + early) * rows, width), f32),
            shape((early * rows, width), bf16),
            shape((rows, half), f32),
            shape((rows, half), bf16),
        ],
        16 * MIB,
        block,
        *parts[:early],
        *beside[:early],
        side,
        side_beside,
        *loaded,
        flops=3 * (2 + 2 * early) * work,
    )
    *first_parts, side = call(
        early_fold_kernel,
        [shape((rows, width), bf16)] * early + [shape((rows, half), bf16)],
        8 * MIB,
        keep,
        swapped(give, 1),
        side_keep,
        swapped(side_give, 1),
    )
    late_keep, late_give = call(
        late_kernel,
        [shape((late * rows, width), f32), shape((late * rows, width), bf16)],
        16 * MIB,
        *parts[early:],
        *beside[early:],
        *loaded,
        flops=6 * late * work,
    )
    folded = call(
        fold_kernel,
        [shape((rows, half), bf16)] * (2 * late),
        8 * MIB,
        late_keep,
        swapped(late_give, 1),
    )
    side = swapped(side, shared)
    first_parts = [swapped(part, *step) for part, step in zip(first_parts, steps)]

    def summed(place):
        parts = [swapped(part, *step) for part, step in zip(folded[place::2], steps[early:])]
        mine, give = call(
            functools.partial(sum_kernel, place, early),
            [shape((rows, piece), f32), shape((rows, piece), bf16)],
            8 * MIB,
            keep,
            side,
            *first_parts,
            *parts,
        )
        return mine, swapped(give, 1)

    distant = call(add_kernel, [shape((rows, piece), bf16)], 4 * MIB, *summed(1))
    distant = swapped(distant, far)
    return call(finish_kernel, [shape((tokens, width), bf16)], 4 * MIB, *summed(0), distant)


def early_count(devices):
    return max(1, (devices // 8 - 1) // 3)


def solution(mesh):
    return jax.shard_map(
        body,
        mesh=mesh,
        in_specs=(
            P(("grp", "ep"), None),
            P(),
            P(("grp", "ep"), None),
            P(("grp", "ep"), None),
            P(("grp", "ep")),
            P("ep", None, None),
            P("ep", None, None),
            P("ep", None, None),
        ),
        out_specs=P(("grp", "ep"), None),
        check_vma=False,
    )
```

```python
import functools
import math

import jax
import jax.numpy as jnp
from jax import lax
from jax.experimental import pallas as pl
from jax.experimental.pallas import tpu as pltpu
from jax.sharding import PartitionSpec as P


VMEM = pl.BlockSpec(memory_space=pltpu.VMEM)
ANY = pl.BlockSpec(memory_space=pl.ANY)
HBM = pl.BlockSpec(memory_space=pltpu.HBM)
PARTS = 4
LOADS = 4
MIB = 1024 * 1024


def swapped(array, *distances):
    size = lax.axis_size("ep")
    pairs = [(i, i ^ distances[i % len(distances)]) for i in range(size)]
    return lax.ppermute(array, "ep", pairs)


def core():
    return lax.rem(lax.axis_index("ep"), 2)


def ordered(own, other):
    first = core() == 0
    return jnp.where(first, own, other), jnp.where(first, other, own)


def wide(ref):
    return ref[...].astype(jnp.float32)


def lane_round(count):
    return -(-count // 128) * 128


def call(kernel, outs, limit, *args, specs=None, flops=0, scratch=()):
    moved = sum(math.prod(a.shape) * a.dtype.itemsize for a in (*args, *outs))
    single = len(outs) == 1
    return pl.pallas_call(
        kernel,
        out_shape=outs[0] if single else tuple(outs),
        in_specs=specs or [VMEM] * len(args),
        out_specs=VMEM if single else tuple([VMEM] * len(outs)),
        scratch_shapes=list(scratch),
        compiler_params=pltpu.CompilerParams(vmem_limit_bytes=limit),
        cost_estimate=pl.CostEstimate(flops=flops, bytes_accessed=moved, transcendentals=0),
    )(*args)


def pack_kernel(
    draft_hbm, states_hbm, gain_hbm, scores_hbm, routes_hbm, out_ref,
    draft_ref, states_ref, gain_ref, scores_ref, routes_ref, sems,
):
    sources = (draft_hbm, states_hbm, gain_hbm, scores_hbm, routes_hbm)
    targets = (draft_ref, states_ref, gain_ref, scores_ref, routes_ref)
    copies = [
        pltpu.make_async_copy(source, target, sems.at[i])
        for i, (source, target) in enumerate(zip(sources, targets))
    ]
    for copy in copies:
        copy.start()
    for copy in copies:
        copy.wait()
    tokens, width = states_ref.shape
    piece = width // PARTS
    extra = out_ref.shape[1] - piece
    requests = draft_ref.shape[0]
    slots = tokens // requests
    states = wide(states_ref)
    mean_square = jnp.mean(states * states, axis=-1, keepdims=True)
    normed = (states * lax.rsqrt(mean_square + 1e-06) * gain_ref[...].reshape(1, width)).astype(jnp.bfloat16)
    scores = scores_ref[...]
    weights = 2.5 * scores / jnp.sum(scores, axis=-1, keepdims=True)
    row = lax.broadcasted_iota(jnp.int32, (tokens, 1), 0)
    live = jnp.zeros((tokens, 1), jnp.bool_)
    for request in range(requests):
        inside = (row >= request * slots) & (row <= request * slots + draft_ref[request])
        live = live | (inside & (row < (request + 1) * slots))
    weights = jnp.where(live, weights, 0.0)
    lane = lax.broadcasted_iota(jnp.int32, (tokens, extra), 1)
    coefficient = jnp.zeros((tokens, extra), jnp.float32)
    for k in range(routes_ref.shape[1]):
        coefficient += jnp.where(routes_ref[:, k : k + 1] == lane, weights[:, k : k + 1], 0.0)
    coarse = coefficient.astype(jnp.bfloat16)
    fine = (coefficient - coarse.astype(jnp.float32)).astype(jnp.bfloat16)
    zero = jnp.zeros((tokens, extra), jnp.float32)
    coarse, fine = coarse.astype(jnp.float32), fine.astype(jnp.float32)
    sides = [coarse, fine] + [zero] * (PARTS - 2)
    normed = normed.astype(jnp.float32)
    normed = jnp.concatenate([normed[:, p * piece : (p + 1) * piece] for p in range(PARTS)], axis=0)
    rows = jnp.concatenate([normed, jnp.concatenate(sides, axis=0)], axis=1).astype(jnp.bfloat16)
    out_ref[...] = rows


def load_kernel(*refs):
    count = (len(refs) - 2) // 2
    token_ref, sems = refs[-2:]
    token_ref[...] = jnp.zeros_like(token_ref)
    copies = []
    for i in range(count):
        source, target = refs[i], refs[count + i]
        step = source.shape[1] // LOADS
        for j in range(LOADS):
            piece = pl.ds(j * step, step)
            copies.append(
                pltpu.make_async_copy(
                    source.at[:, piece], target.at[:, piece], sems.at[i * LOADS + j]
                )
            )
    for copy in copies:
        copy.start()
    for copy in copies:
        copy.wait()


def combine_kernel(own_ref, beside_ref, far_ref, far_beside_ref, after_ref, out_ref, side_ref):
    tokens = own_ref.shape[0] // PARTS
    piece = own_ref.shape[1] - (PARTS * own_ref.shape[1] - out_ref.shape[1]) // 2

    def unfolded(rows):
        parts = [rows[p * tokens : (p + 1) * tokens] for p in range(PARTS)]
        columns = []
        for side in range(2):
            columns += [p[:, :piece] for p in parts[2 * side : 2 * side + 2]]
            columns.append(parts[side][:, piece:])
        return jnp.concatenate(columns, axis=1)

    blocks = ordered(wide(own_ref), wide(beside_ref)) + ordered(wide(far_ref), wide(far_beside_ref))
    rows = jnp.concatenate([unfolded(b) for b in blocks], axis=0)
    out_ref[...] = rows.astype(jnp.bfloat16)
    middle = rows.shape[1] // 2
    side_ref[...] = ordered(rows[:, :middle], rows[:, middle:])[0].astype(jnp.bfloat16)


def hidden_rows(lows, highs, gate_ref, up_ref):
    half = gate_ref.shape[1] // 2
    low, high = jnp.concatenate(lows, axis=0), jnp.concatenate(highs, axis=0)
    mixed = low[:, half:] + high[:, half:]
    lane = lax.broadcasted_iota(jnp.int32, mixed.shape, 1)
    expert = lax.axis_index("ep") // 2
    coefficient = jnp.sum(jnp.where(lane == expert, mixed, 0.0), axis=1, keepdims=True)
    low = low[:, :half].astype(jnp.bfloat16)
    high = high[:, :half].astype(jnp.bfloat16)

    def projected(ref):
        first = jnp.dot(low, ref[0, :half], preferred_element_type=jnp.float32)
        return first + jnp.dot(high, ref[0, half:], preferred_element_type=jnp.float32)

    gate = projected(gate_ref)
    up = projected(up_ref)
    return (gate / (1.0 + jnp.exp(-gate)) * up).astype(jnp.bfloat16), coefficient


def halves(ref):
    middle = ref.shape[1] // 2
    return ref[:, :middle].astype(jnp.float32), ref[:, middle:].astype(jnp.float32)


def lowered(hidden, coefficient, down_ref, first, count):
    columns = down_ref[0, :, first : first + count]
    return jnp.dot(hidden, columns, preferred_element_type=jnp.float32) * coefficient


def early_kernel(*refs):
    *refs, keep_ref, give_ref, side_keep_ref, side_give_ref = refs
    *others, side_ref, side_beside_ref, gate_ref, up_ref, down_ref = refs
    lows, highs = zip(*[halves(ref) for ref in others])
    side_low, side_high = ordered(wide(side_ref), wide(side_beside_ref))
    hidden, coefficient = hidden_rows(
        [*lows, side_low], [*highs, side_high], gate_ref, up_ref
    )
    rows, width = keep_ref.shape
    end = rows + give_ref.shape[0]
    half = width // 2
    step = half // 2
    for start in range(0, half, step):
        low = lowered(hidden, coefficient, down_ref, start, step)
        high = lowered(hidden, coefficient, down_ref, half + start, step)
        for value, first in ((low, start), (high, half + start)):
            keep_ref[:, first : first + step] = value[:rows]
            give_ref[:, first : first + step] = value[rows:end].astype(jnp.bfloat16)
        keep, give = ordered(low[end:], high[end:])
        side_keep_ref[:, start : start + step] = keep
        side_give_ref[:, start : start + step] = give.astype(jnp.bfloat16)


def late_kernel(*refs):
    *others, gate_ref, up_ref, down_ref, keep_ref, give_ref = refs
    lows, highs = zip(*[halves(ref) for ref in others])
    hidden, coefficient = hidden_rows(lows, highs, gate_ref, up_ref)
    rows, width = keep_ref.shape
    step = width // 4
    for start in range(0, width, step):
        partial = lowered(hidden, coefficient, down_ref, start, step)
        keep_ref[:, start : start + step] = partial[:rows]
        give_ref[:, start : start + step] = partial[rows:].astype(jnp.bfloat16)


def early_fold_kernel(*refs):
    keep_ref, other_ref, side_keep_ref, side_other_ref, *outs, side_out_ref = refs
    count = side_out_ref.shape[0]
    side_out_ref[...] = (side_keep_ref[...] + wide(side_other_ref)).astype(jnp.bfloat16)
    for j, out_ref in enumerate(outs):
        total = keep_ref[(j + 1) * count : (j + 2) * count, :]
        total += other_ref[j * count : (j + 1) * count, :].astype(jnp.float32)
        out_ref[...] = total.astype(jnp.bfloat16)


def fold_kernel(keep_ref, other_ref, *outs):
    rows, half = outs[0].shape
    count = rows // 2
    total = keep_ref[...] + wide(other_ref)
    for j, out_ref in enumerate(outs):
        part = total[j * count : (j + 1) * count]
        both = jnp.concatenate([part[:, :half], part[:, half:]], axis=0)
        out_ref[...] = both.astype(jnp.bfloat16)


def sum_kernel(place, early, *refs):
    keep_ref, side_ref, *parts, mine_ref, give_ref = refs
    count, half = side_ref.shape[0] // 2, side_ref.shape[1]
    tokens = count // 2
    piece = half // 2
    rows = slice(place * count, (place + 1) * count)
    total = keep_ref[rows, :]
    for ref in parts[:early]:
        total += wide(ref)[rows]
    total = jnp.concatenate([total[:, :half], total[:, half:]], axis=0)
    side = wide(side_ref)[rows]
    total += jnp.concatenate(ordered(side, jnp.zeros_like(side)), axis=0)
    for ref in parts[early:]:
        total += wide(ref)
    quarters = [total[q * tokens : (q + 1) * tokens] for q in range(4)]
    pairs = [ordered(quarters[0], quarters[1]), ordered(quarters[2], quarters[3])]

    def folded(which):
        pieces = [pair[which][:, c : c + piece] for pair in pairs for c in (0, piece)]
        return jnp.concatenate(pieces, axis=0)

    mine_ref[...] = folded(0)
    give_ref[...] = folded(1).astype(jnp.bfloat16)


def add_kernel(mine_ref, other_ref, out_ref):
    out_ref[...] = (mine_ref[...] + wide(other_ref)).astype(out_ref.dtype)


def finish_kernel(near_ref, beside_ref, other_ref, out_ref):
    tokens, width = out_ref.shape
    piece = width // PARTS
    total = near_ref[...] + wide(beside_ref) + wide(other_ref)
    for p in range(PARTS):
        rows = total[p * tokens : (p + 1) * tokens]
        out_ref[:, p * piece : (p + 1) * piece] = rows.astype(jnp.bfloat16)


def body(hidden_states, norm_gain, gate_scores, routes, draft_counts, w_gate, w_up, w_down):
    tokens, width = hidden_states.shape
    devices = lax.axis_size("ep")
    far = devices // 2
    shared = far - 2
    steps = [(hop, shared ^ hop) for hop in range(2, far // 2, 2)]
    half, piece = width // 2, width // PARTS
    extra = lane_round(far)
    shape = jax.ShapeDtypeStruct
    bf16, f32 = jnp.bfloat16, jnp.float32
    inner = w_gate.shape[2]

    small = [
        pltpu.with_memory_space_constraint(a, pltpu.HBM)
        for a in (draft_counts, hidden_states, norm_gain, gate_scores, routes)
    ]
    packed = call(
        pack_kernel,
        [shape((PARTS * tokens, piece + extra), bf16)],
        4 * MIB,
        *small,
        specs=[HBM] * 5,
        scratch=[pltpu.SMEM(draft_counts.shape, jnp.int32)]
        + [pltpu.VMEM(a.shape, a.dtype) for a in small[1:]]
        + [pltpu.SemaphoreType.DMA((5,))],
    )
    moved = swapped(packed, far)
    beside = swapped(packed, 1)
    weights = [pltpu.with_memory_space_constraint(w, pltpu.HBM) for w in (w_gate, w_up, w_down)]

    def load(*arrays):
        *loaded, token = call(
            load_kernel,
            [pltpu.VMEM(w.shape, w.dtype) for w in arrays] + [shape((8, 128), f32)],
            MIB,
            *arrays,
            specs=[HBM] * len(arrays),
            scratch=[pltpu.SemaphoreType.DMA((len(arrays) * LOADS,))],
        )
        return [pltpu.with_memory_space_constraint(w, pltpu.VMEM) for w in loaded], token

    loaded, token = load(*weights[:2])
    loaded = [*loaded, *load(weights[2])[0]]
    rows = 4 * tokens
    block, side = call(
        combine_kernel,
        [shape((rows, width + 2 * extra), bf16), shape((rows, half + extra), bf16)],
        4 * MIB,
        packed,
        beside,
        moved,
        swapped(moved, 1),
        token,
        specs=[VMEM] * 4 + [ANY],
    )
    side = swapped(side, shared)
    parts = [swapped(block, *step) for step in steps]
    side_beside = swapped(side, 1)
    beside = [swapped(part, 1) for part in parts]
    early = early_count(devices)
    late = len(steps) - early
    work = 2 * rows * width * inner
    keep, give, side_keep, side_give = call(
        early_kernel,
        [
            shape(((1 + early) * rows, width), f32),
            shape((early * rows, width), bf16),
            shape((rows, half), f32),
            shape((rows, half), bf16),
        ],
        16 * MIB,
        block,
        *parts[:early],
        *beside[:early],
        side,
        side_beside,
        *loaded,
        flops=3 * (2 + 2 * early) * work,
    )
    *first_parts, side = call(
        early_fold_kernel,
        [shape((rows, width), bf16)] * early + [shape((rows, half), bf16)],
        8 * MIB,
        keep,
        swapped(give, 1),
        side_keep,
        swapped(side_give, 1),
    )
    late_keep, late_give = call(
        late_kernel,
        [shape((late * rows, width), f32), shape((late * rows, width), bf16)],
        16 * MIB,
        *parts[early:],
        *beside[early:],
        *loaded,
        flops=6 * late * work,
    )
    folded = call(
        fold_kernel,
        [shape((rows, half), bf16)] * (2 * late),
        8 * MIB,
        late_keep,
        swapped(late_give, 1),
    )
    side = swapped(side, shared)
    first_parts = [swapped(part, *step) for part, step in zip(first_parts, steps)]

    def summed(place):
        parts = [swapped(part, *step) for part, step in zip(folded[place::2], steps[early:])]
        mine, give = call(
            functools.partial(sum_kernel, place, early),
            [shape((rows, piece), f32), shape((rows, piece), bf16)],
            8 * MIB,
            keep,
            side,
            *first_parts,
            *parts,
        )
        return mine, swapped(give, 1)

    distant = call(add_kernel, [shape((rows, piece), bf16)], 4 * MIB, *summed(1))
    distant = swapped(distant, far)
    return call(finish_kernel, [shape((tokens, width), bf16)], 4 * MIB, *summed(0), distant)


def early_count(devices):
    return max(1, (devices // 8 - 1) // 3)


def solution(mesh):
    return jax.shard_map(
        body,
        mesh=mesh,
        in_specs=(
            P(("grp", "ep"), None),
            P(),
            P(("grp", "ep"), None),
            P(("grp", "ep"), None),
            P(("grp", "ep")),
            P("ep", None, None),
            P("ep", None, None),
            P("ep", None, None),
        ),
        out_specs=P(("grp", "ep"), None),
        check_vma=False,
    )
```
